32 devices in a mesh: lat: 8 (over y, x, core), lon: 4 (over z).
Axes of the slice: x: 2, y: 2, z: 4, core: 2. Of those that a mesh axis runs over, the one named last changes fastest.
Arguments:
- state: bfloat16 [2, 64, 256, 512], P(None, None, 'lat', 'lon'), may hold values from 3 to 5
- land_mask: int32 [256, 512], P('lat', 'lon'), may hold values from 0 to 1, as said below
- conv_weight: bfloat16 [3, 3, 64, 64], replicated, may hold values from -0.25 to 0.25
- norm_gain: float32 [64], replicated, may hold values from 0.5 to 1.5
- batchnorm_bias: float32 [64], replicated, may hold values from -0.5 to 0.5
- cotangent: bfloat16 [2, 64, 256, 512], P(None, None, 'lat', 'lon'), may hold values from -6 to 6
Outputs:
- activated: bfloat16 [2, 64, 256, 512], P(None, None, 'lat', 'lon')
- state_grad: bfloat16 [2, 64, 256, 512], P(None, None, 'lat', 'lon')
- weight_grad: float32 [3, 3, 64, 64], replicated
- gain_gradient: float32 [64], replicated
- bias_grad: float32 [64], replicated
The draws below stay inside these ranges and needn't reach their ends.
Inputs may be any that keep to these rules, and one draw needn't show every extreme that they name: `land_mask`: ocean pixels lie in whole 32 x 32 ocean blocks, with some land pixels among them; land blocks are all 0. The first block of every region of 32 x 128 pixels is an ocean block.
All inputs are finite; a program needn't handle non-finite values.
Results may differ from the reference program's by a relative error of at most 0.00105.
The reference program's roundings to bfloat16 on the way count: a program that leaves them out, or rounds other values in their place, can miss the bound.
Values may be sent and summed in bfloat16 or wider, within the bound.
No kernel may reach another device: no remote copies, remote signals or barrier semaphores. Data moves between devices by JAX's collectives and lax.ppermute only.
A program may use at most 128 MiB of HBM per device.

```python
import jax
import jax.numpy as jnp
from jax import lax

C = 64
B = 2
BLOCK = 32
ROWS_DEV = 32
COLS_DEV = 128
NLAT_PIX = 256
NLON_PIX = 512


def draw_land_mask(key, part):
    base = jax.random.fold_in(key, 7)
    key_block, key_pixel = jax.random.split(base)
    blocks_lat = NLAT_PIX // BLOCK
    blocks_lon = NLON_PIX // BLOCK
    codes = jax.random.randint(key_block, (blocks_lat, blocks_lon), 0, 16)
    lat_index = jnp.arange(blocks_lat, dtype=jnp.int32)
    lon_index = jnp.arange(blocks_lon, dtype=jnp.int32)
    thresh = 2 + lat_index * 10 // max(blocks_lat - 1, 1)
    ocean_block = (codes >= thresh[:, None]).astype(jnp.int32)
    first_lat = lat_index % (ROWS_DEV // BLOCK) == 0
    first_lon = lon_index % (COLS_DEV // BLOCK) == 0
    forced = jnp.logical_and(first_lat[:, None], first_lon[None, :]).astype(jnp.int32)
    ocean_block = jnp.maximum(ocean_block, forced)
    ocean_block = jnp.repeat(jnp.repeat(ocean_block, BLOCK, axis=0), BLOCK, axis=1)
    pixels = (jax.random.randint(key_pixel, (NLAT_PIX, NLON_PIX), 0, 8) != 0).astype(jnp.int32)
    return ocean_block * pixels


def level_of(rng, dims, shards, least, high):
    factor_of = 1.0
    for axis_at, parts in shards:
        draws = jax.random.uniform(jax.random.fold_in(jax.random.fold_in(rng, 6), axis_at), (parts,), jnp.float32, least / len(shards), high / len(shards))
        factor_of = factor_of * jnp.repeat(jnp.exp(draws), dims[axis_at] // parts).reshape((-1,) + (1,) * (len(dims) - 1 - axis_at))
    return factor_of


def centred(key, shape, scale, most, pieces=(), kind=jnp.bfloat16):
    loudness = level_of(key, shape, pieces, -0.22, 0.18) if pieces else 1.0
    result = jax.random.normal(key, shape, jnp.float32) * scale * loudness
    return jnp.minimum(jnp.maximum(result, -most), most).astype(kind)


def setup_inputs(seed: int = 0) -> dict:
    seeds = jax.random.split(jax.random.key(seed), 7)
    return {
        "state": jnp.clip(3.0 + 2.0 * jax.random.uniform(seeds[0], (B, C, NLAT_PIX, NLON_PIX), jnp.float32) ** level_of(seeds[0], (B, C, NLAT_PIX, NLON_PIX), ((2, 8), (3, 4)), -0.2, 0.2), 3.0, 5.0).astype(jnp.bfloat16),
        "land_mask": draw_land_mask(jax.random.fold_in(seeds[6], 71), 0),
        "conv_weight": centred(seeds[2], (3, 3, C, C), (9 * C) ** -0.5, 0.25),
        "norm_gain": jnp.clip(1.0 + 0.1 * jax.random.normal(seeds[3], (C,), jnp.float32), 0.5, 1.5),
        "batchnorm_bias": jnp.clip(jax.random.uniform(seeds[4], (C,), jnp.float32, -0.5, 0.5), -0.5, 0.5),
        "cotangent": centred(seeds[5], (B, C, NLAT_PIX, NLON_PIX), 1.0, 6.0, ((2, 8), (3, 4))),
    }


def wrap_pad(field):
    wrapped = jnp.concatenate([field[..., -1:], field, field[..., :1]], axis=3)
    zeros = jnp.zeros(wrapped.shape[:2] + (1, wrapped.shape[3]), wrapped.dtype)
    return jnp.concatenate([zeros, wrapped, zeros], axis=2)

def valid_conv(padded, kernel):
    return lax.conv_general_dilated(padded, kernel, (1, 1), 'VALID', dimension_numbers=('NCHW', 'HWIO', 'NCHW'), preferred_element_type=jnp.float32)

def kernel_grad(padded, grad):
    raw = lax.conv_general_dilated(padded, grad, (1, 1), 'VALID', dimension_numbers=('CNHW', 'IOHW', 'NCHW'), preferred_element_type=jnp.float32)
    return jnp.transpose(raw, (2, 3, 0, 1))

def reference(state, land_mask, conv_weight, norm_gain, batchnorm_bias, cotangent):
    maskf = land_mask.astype(jnp.float32)
    full_ocean_mask = maskf[None, None]
    masked = state * land_mask.astype(jnp.bfloat16)[None, None]
    padded = wrap_pad(masked)
    conv = valid_conv(padded, conv_weight)
    count = jnp.maximum(state.shape[0] * jnp.sum(maskf), 1.0)
    mean = lax.optimization_barrier(jnp.sum(conv * full_ocean_mask, axis=(0, 2, 3))) / count
    centered_deviation = conv - mean[None, :, None, None]
    var = lax.optimization_barrier(jnp.sum(centered_deviation * centered_deviation * full_ocean_mask, axis=(0, 2, 3))) / count
    inverse_stddev = lax.rsqrt(var + 1e-05)
    normalized_state = centered_deviation * inverse_stddev[None, :, None, None]
    batchnorm_gain = norm_gain[None, :, None, None]
    preactivation = batchnorm_gain * normalized_state + batchnorm_bias[None, :, None, None]
    sigmoid_pre = jax.nn.sigmoid(preactivation)
    activated = (preactivation * sigmoid_pre * full_ocean_mask).astype(jnp.bfloat16)
    slope = sigmoid_pre * (1.0 + preactivation * (1.0 - sigmoid_pre))
    preactivation_gradient = cotangent.astype(jnp.float32) * full_ocean_mask * slope
    bias_grad = lax.optimization_barrier(jnp.sum(preactivation_gradient, axis=(0, 2, 3)))
    gain_gradient = lax.optimization_barrier(jnp.sum(preactivation_gradient * normalized_state, axis=(0, 2, 3)))
    shifted_first = (norm_gain * bias_grad / count)[None, :, None, None]
    shifted_second = (norm_gain * gain_gradient / count)[None, :, None, None]
    convolution_gradient_map = (full_ocean_mask * inverse_stddev[None, :, None, None] * (batchnorm_gain * preactivation_gradient - shifted_first - normalized_state * shifted_second)).astype(jnp.bfloat16)
    weight_grad = kernel_grad(padded, convolution_gradient_map)
    flipped = jnp.transpose(conv_weight[::-1, ::-1], (0, 1, 3, 2))
    back = valid_conv(wrap_pad(convolution_gradient_map), flipped)
    state_grad = (back * full_ocean_mask).astype(jnp.bfloat16)
    return (activated, state_grad, weight_grad, gain_gradient, bias_grad)
```

```python
import functools

import jax
import jax.numpy as jnp
from jax import lax
from jax.experimental import pallas as pl
from jax.experimental.pallas import tpu as pltpu
from jax.sharding import PartitionSpec as P

F32 = jnp.float32
BF16 = jnp.bfloat16
STEP = 2
EPS = 1e-05


def lane_of(rows, width):
    return lax.broadcasted_iota(jnp.int32, (rows, width), 1)


def rolled(value, shift, width):
    return pltpu.roll(value, lax.rem(shift + 4 * width, width), 1)


def any_lane(lane, picks):
    hit = lane == picks[0]
    for p in picks[1:]:
        hit = jnp.logical_or(hit, lane == p)
    return hit


def call(kernel, out_shape, scratch, flops, nbytes, *args):
    return pl.pallas_call(
        kernel,
        out_shape=out_shape,
        scratch_shapes=scratch,
        compiler_params=pltpu.CompilerParams(vmem_limit_bytes=24 << 20),
        cost_estimate=pl.CostEstimate(flops=flops, bytes_accessed=nbytes, transcendentals=0),
    )(*args)


def spread_rows(src_ref, tmp, chunk, mask):
    batch, chans, high, width = src_ref.shape
    for b in range(batch):
        for c0 in range(0, chans, chunk):
            part = src_ref[b, c0 : c0 + chunk].astype(F32)
            if mask is not None:
                part = part * mask[None]
            at = (b * chans + c0) * high
            tmp[at : at + chunk * high, :] = part.reshape(chunk * high, width)


def gather_kernel(x_ref, mask_ref, xm_ref, top_ref, bot_ref, sl_ref, sr_ref, tmp):
    batch, chans, high, width = x_ref.shape
    mask = mask_ref[...].astype(F32)
    spread_rows(x_ref, tmp, 8, mask)
    lane = lane_of(chans, width)
    sl = jnp.zeros((chans, width), F32)
    sr = jnp.zeros((chans, width), F32)
    for b in range(batch):

        def row(h, carry, b=b):
            sl, sr = carry
            v = tmp[pl.ds(b * chans * high + h, chans, stride=high), :]
            xm_ref[b, :, pl.ds(pl.multiple_of(h * width, width), width)] = v.astype(BF16)
            i = b * high + h
            sl = jnp.where(lane == lax.rem(2 * i - 1 + width, width), rolled(v, 2 * i - 1, width), sl)
            sr = jnp.where(lane == 2 * i, rolled(v, 2 * i + 1, width), sr)
            return sl, sr

        sl, sr = lax.fori_loop(0, high, row, (sl, sr), unroll=4)
        top_ref[b] = xm_ref[b, :, 0:width]
        bot_ref[b] = xm_ref[b, :, (high - 1) * width : high * width]
    sl_ref[...] = sl.astype(BF16)
    sr_ref[...] = sr.astype(BF16)


def relay_kernel(x_ref, out_ref, tmp):
    batch, chans, high, width = x_ref.shape
    spread_rows(x_ref, tmp, 8, None)
    for b in range(batch):

        def row(h, carry, b=b):
            v = tmp[pl.ds(b * chans * high + h, chans, stride=high), :]
            out_ref[b, :, pl.ds(pl.multiple_of(h * width, width), width)] = v.astype(BF16)
            return carry

        lax.fori_loop(0, high, row, 0, unroll=4)


def corner_kernel(high, batch, top_ref, bot_ref, fl_ref, fr_ref, edge_ref, up_ref, dn_ref):
    chans, width = fl_ref.shape
    lane = lane_of(chans, width)
    edge = fl_ref[...].astype(F32) + fr_ref[...].astype(F32)
    far = 2 * (high - 1)
    low = [2 * b * high + d for b in range(batch) for d in (0, -1)]
    low = [p % width for p in low]
    tall = [(p + far) % width for p in low]
    edge_ref[...] = edge.astype(BF16)
    up = jnp.where(any_lane(lane, tall), rolled(edge, far, width), 0.0)
    dn = jnp.where(any_lane(lane, low), rolled(edge, -far, width), 0.0)
    for b in range(batch):
        up_ref[b] = top_ref[b]
        dn_ref[b] = bot_ref[b]
    up_ref[batch] = up.astype(BF16)
    dn_ref[batch] = dn.astype(BF16)


def edge_stack(edge_ref, above_ref, below_ref, high, batch):
    chans, width = edge_ref.shape
    lane = lane_of(chans, width)
    edge = edge_ref[...].astype(F32)
    far = 2 * (high - 1)
    low = [(2 * b * high + d) % width for b in range(batch) for d in (0, -1)]
    tall = [(p + far) % width for p in low]
    first = jnp.where(any_lane(lane, low), above_ref[batch].astype(F32), rolled(edge, 2, width))
    last = jnp.where(any_lane(lane, tall), below_ref[batch].astype(F32), rolled(edge, -2, width))
    return jnp.concatenate([first, edge, last], axis=0).astype(BF16)


def fill_padded(pad_ref, x_ref, above_ref, below_ref, width):
    batch, chans, flat = x_ref.shape
    for b in range(batch):
        pad_ref[b, :, 0:width] = above_ref[b]
        pad_ref[b, :, width : width + flat] = x_ref[b]
        pad_ref[b, :, width + flat :] = below_ref[b]


def conv_rows(pad_ref, w_ref, fix, b, j, high, width, lane):
    n = STEP * width
    rhs = jnp.concatenate(
        [pad_ref[b, :, pl.ds(pl.multiple_of((j + ky) * width, width), n)] for ky in range(3)], axis=0
    )
    y = jnp.dot(w_ref[...], rhs, preferred_element_type=F32)
    c = y.shape[0] // 3
    rows = []
    for r in range(STEP):
        i = b * high + j + r
        y0 = y[0:c, r * width : (r + 1) * width]
        y1 = y[c : 2 * c, r * width : (r + 1) * width]
        y2 = y[2 * c :, r * width : (r + 1) * width]
        g = rolled(fix, -2 * i, width)
        left = jnp.where(lane == 0, g, rolled(y0, 1, width))
        right = jnp.where(lane == width - 1, g, rolled(y2, -1, width))
        rows.append(left + y1 + right)
    return rows


def edge_fix(w_ref, stack, lane):
    g = jnp.dot(w_ref[...], stack, preferred_element_type=F32)
    c = g.shape[0] // 3
    return jnp.where(lax.rem(lane, 2) == 0, g[0:c], g[2 * c :])


def lanes_sum(first, second):
    both = jnp.concatenate([first, second], axis=0)
    return jnp.sum(jnp.transpose(both), axis=0, keepdims=True)


def conv_kernel(
    x_ref, above_ref, below_ref, edge_ref, w_ref, mask_ref, conv_ref, pad_ref, stack_ref, stat_ref, maskf
):
    batch, chans, flat = x_ref.shape
    high, width = mask_ref.shape
    lane = lane_of(chans, width)
    maskf[...] = mask_ref[...].astype(F32)
    fill_padded(pad_ref, x_ref, above_ref, below_ref, width)
    stack = edge_stack(edge_ref, above_ref, below_ref, high, batch)
    stack_ref[...] = stack
    fix = edge_fix(w_ref, stack, lane)
    total = jnp.zeros((chans, width), F32)
    for b in range(batch):

        def step(k, total, b=b):
            j = k * STEP
            rows = conv_rows(pad_ref, w_ref, fix, b, j, high, width, lane)
            for r, out in enumerate(rows):
                conv_ref[b, :, pl.ds(pl.multiple_of((j + r) * width, width), width)] = out
                total = total + out * maskf[pl.ds(j + r, 1), :]
            return total

        total = lax.fori_loop(0, high // STEP, step, total, unroll=2)
    n = batch * jnp.sum(maskf[...])
    mean = jnp.sum(total, axis=1, keepdims=True) / jnp.maximum(n, 1.0)
    mean = jnp.broadcast_to(mean, (chans, width))
    spread = jnp.zeros((chans, width), F32)
    for b in range(batch):

        def step(h, spread, b=b):
            dev = conv_ref[b, :, pl.ds(pl.multiple_of(h * width, width), width)] - mean
            return spread + dev * dev * maskf[pl.ds(h, 1), :]

        spread = lax.fori_loop(0, high, step, spread, unroll=4)
    stat_ref[0:1, :] = lanes_sum(total, spread)
    stat_ref[1:2, :] = jnp.full((1, 2 * chans), n, F32)


def columns(rows, chans):
    width = rows[0].shape[1]
    pad = jnp.zeros((width - len(rows), width), F32)
    return jnp.transpose(jnp.concatenate(rows + [pad], axis=0))[0:chans]


def column(cols, k, width):
    return jnp.broadcast_to(cols[:, k : k + 1], (cols.shape[0], width))


def silu_kernel(stat_ref, conv_ref, cot_ref, mask_ref, gb_ref, act_ref, dpre_ref, par_ref, sum_ref, maskf, tmp):
    batch, chans, flat = conv_ref.shape
    high, width = mask_ref.shape
    maskf[...] = mask_ref[...].astype(F32)
    stat = stat_ref[:, 0, :]
    n = stat_ref[:, 1, :]
    count = jnp.maximum(jnp.sum(n, axis=0, keepdims=True), 1.0)
    both = jnp.sum(stat, axis=0, keepdims=True)
    mean = both / count
    off = stat / jnp.maximum(n, 1.0) - mean
    between = jnp.sum(n * off * off, axis=0, keepdims=True)
    var = (rolled(both, chans, width) + between) / count
    inv = lax.rsqrt(var + EPS)
    gain, bias = gb_ref[0:1, :], gb_ref[1:2, :]
    par_ref[...] = columns([mean, inv, gain, bias, count], chans)
    cols = par_ref[...]
    mean, inv, gain, bias = (column(cols, k, width) for k in range(4))
    sums = (jnp.zeros((chans, width), F32), jnp.zeros((chans, width), F32))
    for b in range(batch):

        def row(h, sums, b=b):
            at = pl.ds(pl.multiple_of(h * width, width), width)
            m = maskf[pl.ds(h, 1), :]
            xhat = (conv_ref[b, :, at] - mean) * inv
            pre = gain * xhat + bias
            s = 0.5 + 0.5 * jnp.tanh(0.5 * pre)
            tmp[pl.ds(b * chans * high + h, chans, stride=high), :] = pre * s * m
            dpre = cot_ref[b, :, at].astype(F32) * m * (s * (1.0 + pre * (1.0 - s)))
            dpre_ref[b, :, at] = dpre
            return sums[0] + dpre, sums[1] + dpre * xhat

        sums = lax.fori_loop(0, high, row, sums, unroll=2)
    sum_ref[...] = lanes_sum(*sums)
    pack_rows(tmp, act_ref, 8)


def pack_rows(tmp, out_ref, chunk):
    batch, chans, high, width = out_ref.shape
    for b in range(batch):
        for c0 in range(0, chans, chunk):
            at = (b * chans + c0) * high
            out_ref[b, c0 : c0 + chunk] = (
                tmp[at : at + chunk * high, :].astype(BF16).reshape(chunk, high, width)
            )


def grad_kernel(
    sum_ref, conv_ref, dpre_ref, par_ref, pad_ref, stack_ref, mask_ref,
    d_ref, top_ref, bot_ref, sl_ref, sr_ref, wg_ref, gg_ref, maskf, acc,
):
    batch, chans, flat = conv_ref.shape
    high, width = mask_ref.shape
    lane = lane_of(chans, width)
    maskf[...] = mask_ref[...].astype(F32)
    both = jnp.sum(sum_ref[:, 0, :], axis=0, keepdims=True)
    gg_ref[...] = both
    cols = par_ref[...]
    mean, inv, gain, count = (column(cols, k, width) for k in (0, 1, 2, 4))
    sums = columns([both], 2 * chans)
    first = gain * column(sums[0:chans], 0, width) / count
    second = gain * column(sums[chans:], 0, width) / count
    acc[...] = jnp.zeros_like(acc)
    sl = jnp.zeros((chans, width), F32)
    sr = jnp.zeros((chans, width), F32)
    contract = (((1,), (1,)), ((), ()))
    for b in range(batch):

        def step(k, carry, b=b):
            sl, sr = carry
            j = k * STEP
            stacks = []
            for r in range(STEP):
                h = j + r
                at = pl.ds(pl.multiple_of(h * width, width), width)
                m = maskf[pl.ds(h, 1), :]
                xhat = (conv_ref[b, :, at] - mean) * inv
                d = m * inv * (gain * dpre_ref[b, :, at] - first - xhat * second)
                d = d.astype(BF16)
                d_ref[b, :, at] = d
                v = d.astype(F32)
                i = b * high + h
                sl = jnp.where(lane == lax.rem(2 * i - 1 + width, width), rolled(v, 2 * i - 1, width), sl)
                sr = jnp.where(lane == 2 * i, rolled(v, 2 * i + 1, width), sr)
                back = jnp.where(lane == width - 1, 0.0, rolled(v, -1, width)).astype(BF16)
                forth = jnp.where(lane == 0, 0.0, rolled(v, 1, width)).astype(BF16)
                stacks.append(jnp.concatenate([back, d, forth], axis=0))
            taps = jnp.concatenate(
                [
                    pad_ref[b, :, pl.ds(pl.multiple_of((j + ky) * width, width), STEP * width)]
                    for ky in range(3)
                ],
                axis=0,
            )
            acc[...] += lax.dot_general(
                taps, jnp.concatenate(stacks, axis=1), contract, preferred_element_type=F32
            )
            return sl, sr

        sl, sr = lax.fori_loop(0, high // STEP, step, (sl, sr), unroll=2)
        top_ref[b] = d_ref[b, :, 0:width]
        bot_ref[b] = d_ref[b, :, (high - 1) * width : high * width]
    sl_ref[...] = sl.astype(BF16)
    sr_ref[...] = sr.astype(BF16)
    rim = jnp.concatenate(
        [rolled(sl, 1, width), jnp.zeros((chans, width), F32), rolled(sr, -1, width)], axis=0
    ).astype(BF16)
    full = acc[...] + lax.dot_general(stack_ref[...], rim, contract, preferred_element_type=F32)
    half = 3 * chans // 2
    wg_ref[0 : 3 * chans, :] = full[:, 0 : 2 * chans]
    wg_ref[3 * chans :, :] = jnp.concatenate([full[0:half, 2 * chans :], full[half:, 2 * chans :]], axis=1)


def unpack_kernel(chans, wg_ref, out_ref):
    half = 3 * chans // 2
    for ky in range(3):
        for kx in range(2):
            out_ref[ky, kx] = wg_ref[ky * chans : (ky + 1) * chans, kx * chans : (kx + 1) * chans]
    tail = jnp.concatenate(
        [wg_ref[3 * chans :, 0:chans], wg_ref[3 * chans :, chans : 2 * chans]], axis=0
    )
    for ky in range(3):
        out_ref[ky, 2] = tail[ky * chans : (ky + 1) * chans]


def back_kernel(d_ref, above_ref, below_ref, edge_ref, w_ref, mask_ref, out_ref, pad_ref, maskf, tmp):
    batch, chans, flat = d_ref.shape
    high, width = mask_ref.shape
    lane = lane_of(chans, width)
    maskf[...] = mask_ref[...].astype(F32)
    fill_padded(pad_ref, d_ref, above_ref, below_ref, width)
    fix = edge_fix(w_ref, edge_stack(edge_ref, above_ref, below_ref, high, batch), lane)
    for b in range(batch):

        def step(k, carry, b=b):
            j = k * STEP
            rows = conv_rows(pad_ref, w_ref, fix, b, j, high, width, lane)
            for r, out in enumerate(rows):
                tmp[pl.ds(b * chans * high + j + r, chans, stride=high), :] = out * maskf[pl.ds(j + r, 1), :]
            return carry

        lax.fori_loop(0, high // STEP, step, 0, unroll=2)
    pack_rows(tmp, out_ref, 8)


def to_all(row, axes):
    count = lax.axis_size(axes)
    tiled = jnp.broadcast_to(row[None], (count,) + row.shape)
    return lax.all_to_all(tiled, axes, 0, 0)


def lon_swap(sl, sr):
    n = lax.axis_size("lon")
    from_left = lax.ppermute(sr, "lon", [(i, (i + 1) % n) for i in range(n)])
    from_right = lax.ppermute(sl, "lon", [((i + 1) % n, i) for i in range(n)])
    return from_left, from_right


def lat_swap(up, dn):
    n = lax.axis_size("lat")
    above = lax.ppermute(dn, "lat", [(i, i + 1) for i in range(n - 1)])
    below = lax.ppermute(up, "lat", [(i + 1, i) for i in range(n - 1)])
    return above, below


def halos(top, bot, sl, sr, high):
    batch, chans, width = top.shape
    from_left, from_right = lon_swap(sl, sr)
    shapes = (
        jax.ShapeDtypeStruct((chans, width), BF16),
        jax.ShapeDtypeStruct((batch + 1, chans, width), BF16),
        jax.ShapeDtypeStruct((batch + 1, chans, width), BF16),
    )
    edge, up, dn = call(
        functools.partial(corner_kernel, high, batch), shapes, [], 0, 200_000, top, bot, from_left, from_right
    )
    above, below = lat_swap(up, dn)
    return above, below, edge


def pairwise(x, axis, bit):
    n = lax.axis_size(axis)
    return x + lax.ppermute(x, axis, [(i, i ^ bit) for i in range(n)])


def bits_of(axis):
    n = lax.axis_size(axis)
    return [(axis, 1 << k) for k in range(n.bit_length() - 1)]


def sum_everywhere(x):
    sizes = [lax.axis_size(a) for a in ("lat", "lon")]
    if any(n & (n - 1) for n in sizes) or sizes[0] < 2:
        return lax.psum(x, ("lat", "lon"))
    half = x.shape[0] // 2
    n = sizes[0]
    odd = lax.axis_index("lat") % 2 == 1
    keep = jnp.where(odd, x[half:], x[:half])
    give = jnp.where(odd, x[:half], x[half:])
    swap = [(i, i ^ 1) for i in range(n)]
    part = keep + lax.ppermute(give, "lat", swap)
    steps = bits_of("lat")[1:] + bits_of("lon")
    for axis, bit in steps:
        part = pairwise(part, axis, bit)
    other = lax.ppermute(part, "lat", swap)
    return jnp.concatenate([jnp.where(odd, other, part), jnp.where(odd, part, other)], axis=0)


def on_device(state, land_mask, conv_weight, norm_gain, batchnorm_bias, cotangent):
    batch, chans, high, width = state.shape
    flat = high * width
    axes = ("lat", "lon")
    S = jax.ShapeDtypeStruct
    mat = 2 * batch * flat * 9 * chans * chans
    size = batch * chans * flat * 2
    tmp = pltpu.VMEM((batch * chans * high, width), F32)
    maskf = pltpu.VMEM((high, width), F32)
    plane = S((batch, chans, flat), BF16)
    rows = S((batch, chans, width), BF16)
    cols = S((chans, width), BF16)
    xm, top, bot, sl, sr = call(
        gather_kernel, (plane, rows, rows, cols, cols), [tmp], 0, 2 * size, state, land_mask
    )
    cot = call(relay_kernel, plane, [tmp], 0, 2 * size, cotangent)
    w_fwd = jnp.transpose(conv_weight, (1, 3, 0, 2)).reshape(3 * chans, 3 * chans)
    w_back = jnp.transpose(conv_weight[::-1, ::-1], (1, 2, 0, 3)).reshape(3 * chans, 3 * chans)
    gb = jnp.pad(jnp.stack([norm_gain, batchnorm_bias]), ((0, 0), (0, width - chans)))
    above, below, edge = halos(top, bot, sl, sr, high)
    conv, padded, stack, stat = call(
        conv_kernel,
        (
            S((batch, chans, flat), F32),
            S((batch, chans, flat + 2 * width), BF16),
            S((3 * chans, width), BF16),
            S((2, 2 * chans), F32),
        ),
        [maskf],
        mat,
        4 * size,
        xm, above, below, edge, w_fwd, land_mask,
    )
    stats = to_all(stat, axes)
    activated, dpre, par, sums = call(
        silu_kernel,
        (
            S(state.shape, BF16),
            S((batch, chans, flat), F32),
            S((chans, width), F32),
            S((1, 2 * chans), F32),
        ),
        [maskf, tmp],
        20 * size,
        6 * size,
        stats, conv, cot, land_mask, gb,
    )
    sums = to_all(sums, axes)
    dmap, top, bot, sl, sr, wg, gg = call(
        grad_kernel,
        (plane, rows, rows, cols, cols, S((9 * chans // 2, 2 * chans), F32), S((1, 2 * chans), F32)),
        [maskf, pltpu.VMEM((3 * chans, 3 * chans), F32)],
        mat,
        6 * size,
        sums, conv, dpre, par, padded, stack, land_mask,
    )
    above, below, edge = halos(top, bot, sl, sr, high)
    state_grad = call(
        back_kernel,
        S(state.shape, BF16),
        [pltpu.VMEM((batch, chans, flat + 2 * width), BF16), maskf, tmp],
        mat,
        3 * size,
        dmap, above, below, edge, w_back, land_mask,
    )
    wg = sum_everywhere(wg)
    weight_grad = call(
        functools.partial(unpack_kernel, chans), S((3, 3, chans, chans), F32), [], 0, 500_000, wg
    )
    return (activated, state_grad, weight_grad, gg[0, chans:], gg[0, :chans])


def solution(mesh):
    return jax.shard_map(
        on_device,
        mesh=mesh,
        in_specs=(
            P(None, None, "lat", "lon"),
            P("lat", "lon"),
            P(),
            P(),
            P(),
            P(None, None, "lat", "lon"),
        ),
        out_specs=(P(None, None, "lat", "lon"), P(None, None, "lat", "lon"), P(), P(), P()),
        check_vma=False,
    )
```

```python
import functools

import jax
import jax.numpy as jnp
from jax import lax
from jax.experimental import pallas as pl
from jax.experimental.pallas import tpu as pltpu
from jax.sharding import PartitionSpec as P

F32 = jnp.float32
BF16 = jnp.bfloat16
STEP = 2
CHUNK = 16
GROUP = 4
EPS = 1e-05


def lane_of(rows, width):
    return lax.broadcasted_iota(jnp.int32, (rows, width), 1)


def rolled(value, shift, width):
    return pltpu.roll(value, lax.rem(shift + 4 * width, width), 1)


def any_lane(lane, picks):
    hit = lane == picks[0]
    for p in picks[1:]:
        hit = jnp.logical_or(hit, lane == p)
    return hit


def call(kernel, out_shape, scratch, flops, nbytes, *args, fetch=False):
    space = pl.ANY if fetch else pltpu.VMEM
    return pl.pallas_call(
        kernel,
        out_shape=out_shape,
        in_specs=[pl.BlockSpec(memory_space=space)] * len(args),
        scratch_shapes=scratch,
        compiler_params=pltpu.CompilerParams(vmem_limit_bytes=24 << 20),
        cost_estimate=pl.CostEstimate(flops=flops, bytes_accessed=nbytes, transcendentals=0),
    )(*args)


def flags(mask_ref):
    return mask_ref[...].astype(F32)


def row_lanes(h, width, count=1):
    return pl.ds(pl.multiple_of(h * width, width), count * width)


def fetches(src_ref, buf, sems):
    batch, chans = src_ref.shape[:2]
    spots = [(b, c) for b in range(batch) for c in range(0, chans, CHUNK)]
    copies = []
    for n, (b, c) in enumerate(spots):
        part = (b, pl.ds(c, CHUNK))
        copies.append(pltpu.make_async_copy(src_ref.at[part], buf.at[part], sems.at[n]))
    return spots, copies


def spread_rows(src_ref, buf, sems, mask_ref, mbuf, msem, tmp):
    batch, chans, high, width = src_ref.shape
    head = pltpu.make_async_copy(mask_ref, mbuf, msem)
    head.start()
    spots, copies = fetches(src_ref, buf, sems)
    for copy in copies:
        copy.start()
    head.wait()
    mask = flags(mbuf)
    for (b, c0), copy in zip(spots, copies):
        copy.wait()
        for c in range(c0, c0 + CHUNK):
            at = (b * chans + c) * (high + 1)
            tmp[at : at + high, :] = buf[b, c].astype(F32) * mask


def channel_rows(tmp, b, h, chans, high):
    return pl.ds(b * chans * (high + 1) + h, chans, stride=high + 1)


def pack_rows(tmp, out, chans, high):
    for c in range(chans):
        at = c * (high + 1)
        out[c] = tmp[at : at + high, :].astype(BF16)


def packed(old, v, i, lane):
    width = lane.shape[1]
    here = jnp.logical_or(lane == 2 * i, lane == lax.rem(2 * i - 1 + width, width))
    return jnp.where(here, rolled(v, 2 * i, width), old)


def gather_kernel(x_ref, mask_ref, xm_ref, top_ref, bot_ref, side_ref, tmp, buf, mbuf, sems, msem):
    batch, chans, high, width = x_ref.shape
    spread_rows(x_ref, buf, sems, mask_ref, mbuf, msem, tmp)
    lane = lane_of(chans, width)
    side = jnp.zeros((chans, width), F32)
    for b in range(batch):

        def row(h, side, b=b):
            v = tmp[channel_rows(tmp, b, h, chans, high), :]
            xm_ref[b, :, row_lanes(h, width)] = v.astype(BF16)
            return packed(side, v, b * high + h, lane)

        side = lax.fori_loop(0, high, row, side, unroll=8)
        top_ref[b] = xm_ref[b, :, 0:width]
        bot_ref[b] = xm_ref[b, :, (high - 1) * width : high * width]
    side_ref[...] = side.astype(BF16)


def relay_kernel(x_ref, mask_ref, w_hbm, out_ref, fwd_ref, back_ref, tmp, buf, mbuf, sems, msem, w_ref, wsem):
    batch, chans, high, width = x_ref.shape
    weights = pltpu.make_async_copy(w_hbm, w_ref, wsem)
    weights.start()
    spread_rows(x_ref, buf, sems, mask_ref, mbuf, msem, tmp)
    weights.wait()
    for kx in range(3):
        part = jnp.concatenate([w_ref[ky, kx].astype(F32) for ky in range(3)], axis=0)
        fwd_ref[kx * chans : (kx + 1) * chans, :] = jnp.transpose(part).astype(BF16)
        part = [w_ref[2 - ky, 2 - kx].astype(F32) for ky in range(3)]
        back_ref[kx * chans : (kx + 1) * chans, :] = jnp.concatenate(part, axis=1).astype(BF16)
    for b in range(batch):

        def row(h, carry, b=b):
            out_ref[b, :, row_lanes(h, width)] = tmp[channel_rows(tmp, b, h, chans, high), :].astype(BF16)
            return carry

        lax.fori_loop(0, high, row, 0, unroll=8)


def corners(high, batch, width):
    first = [(2 * b * high + d) % width for b in range(batch) for d in (0, -1)]
    return first, [(p + 2 * (high - 1)) % width for p in first]


def corner_kernel(high, batch, top_ref, bot_ref, fl_ref, fr_ref, edge_ref, up_ref, dn_ref):
    chans, width = fl_ref.shape
    lane = lane_of(chans, width)
    even = lax.rem(lane, 2) == 0
    edge = jnp.where(
        even, rolled(fl_ref[...].astype(F32), 1, width), rolled(fr_ref[...].astype(F32), -1, width)
    )
    first, last = corners(high, batch, width)
    far = 2 * (high - 1)
    edge_ref[...] = edge.astype(BF16)
    up = jnp.where(any_lane(lane, last), rolled(edge, far, width), 0.0)
    dn = jnp.where(any_lane(lane, first), rolled(edge, -far, width), 0.0)
    for b in range(batch):
        up_ref[b] = top_ref[b]
        dn_ref[b] = bot_ref[b]
    up_ref[batch] = up.astype(BF16)
    dn_ref[batch] = dn.astype(BF16)


def edge_stack(edge_ref, above_ref, below_ref, high, batch):
    chans, width = edge_ref.shape
    lane = lane_of(chans, width)
    edge = edge_ref[...].astype(F32)
    first, last = corners(high, batch, width)
    top = jnp.where(any_lane(lane, first), above_ref[batch].astype(F32), rolled(edge, 2, width))
    bottom = jnp.where(any_lane(lane, last), below_ref[batch].astype(F32), rolled(edge, -2, width))
    return jnp.concatenate([top, edge, bottom], axis=0).astype(BF16)


def fill_padded(pad_ref, x_ref, above_ref, below_ref, width, planes):
    flat = x_ref.shape[2]
    for to, b in enumerate(planes):
        pad_ref[to, :, 0:width] = above_ref[b]
        pad_ref[to, :, width : width + flat] = x_ref[b]
        pad_ref[to, :, width + flat :] = below_ref[b]


def taps(pad_ref, b, j, width, count):
    return jnp.concatenate([pad_ref[b, :, row_lanes(j + ky, width, count)] for ky in range(3)], axis=0)


def edge_fix(w_ref, stack, lane):
    g = jnp.dot(w_ref[...], stack, preferred_element_type=F32)
    c = g.shape[0] // 3
    return jnp.where(lax.rem(lane, 2) == 0, g[0:c], g[2 * c :])


def conv_loop(pad_ref, w_ref, bufs, fix, first, high, lane, post, carry):
    planes = pad_ref.shape[0]
    chans, width = lane.shape
    per = high // STEP
    steps = planes * per

    def product(k, buf):
        k = jnp.minimum(k, steps - 1)
        b, j = lax.div(k, per), lax.rem(k, per) * STEP
        buf[...] = jnp.dot(w_ref[...], taps(pad_ref, b, j, width, STEP), preferred_element_type=F32)

    def finish(k, buf, carry):
        b, j = lax.div(k, per), lax.rem(k, per) * STEP
        for r in range(STEP):
            cut = slice(r * width, (r + 1) * width)
            g = rolled(fix, -2 * ((first + b) * high + j + r), width)
            left = jnp.where(lane == 0, g, rolled(buf[0:chans, cut], 1, width))
            right = jnp.where(lane == width - 1, g, rolled(buf[2 * chans :, cut], -1, width))
            carry = post(b, j + r, left + buf[chans : 2 * chans, cut] + right, carry)
        return carry

    def four(p, carry):
        k = 4 * p
        product(k + 2, bufs[2])
        product(k + 3, bufs[3])
        carry = finish(k, bufs[0], carry)
        carry = finish(k + 1, bufs[1], carry)
        product(k + 4, bufs[0])
        product(k + 5, bufs[1])
        carry = finish(k + 2, bufs[2], carry)
        return finish(k + 3, bufs[3], carry)

    product(0, bufs[0])
    product(1, bufs[1])
    return lax.fori_loop(0, steps // 4, four, carry)


def lanes_sum(first, second):
    both = jnp.concatenate([first, second], axis=0)
    return jnp.sum(jnp.transpose(both), axis=0, keepdims=True)


def conv_kernel(
    x_ref, above_ref, below_ref, edge_ref, w_ref, mask_ref,
    conv_ref, pad_ref, stack_ref, stat_ref, maskf, *bufs,
):
    batch, chans, flat = x_ref.shape
    high, width = mask_ref.shape
    lane = lane_of(chans, width)
    maskf[...] = flags(mask_ref)
    fill_padded(pad_ref, x_ref, above_ref, below_ref, width, range(batch))
    stack = edge_stack(edge_ref, above_ref, below_ref, high, batch)
    stack_ref[...] = stack
    fix = edge_fix(w_ref, stack, lane)

    def post(b, h, value, total):
        conv_ref[b, :, row_lanes(h, width)] = value
        return total + value * maskf[pl.ds(h, 1), :]

    zero = jnp.zeros((chans, width), F32)
    total = conv_loop(pad_ref, w_ref, bufs, fix, 0, high, lane, post, zero)
    n = batch * jnp.sum(maskf[...])
    mean = jnp.sum(total, axis=1, keepdims=True) / jnp.maximum(n, 1.0)
    mean = jnp.broadcast_to(mean, (chans, width))
    spread = zero
    for b in range(batch):

        def step(h, spread, b=b):
            dev = conv_ref[b, :, row_lanes(h, width)] - mean
            return spread + dev * dev * maskf[pl.ds(h, 1), :]

        spread = lax.fori_loop(0, high, step, spread, unroll=8)
    copies = stat_ref.shape[0]
    stat_ref[:, 0:1, :] = jnp.broadcast_to(lanes_sum(total, spread)[None], (copies, 1, 2 * chans))
    stat_ref[:, 1:2, :] = jnp.full((copies, 1, 2 * chans), n, F32)


def columns(rows, chans):
    width = rows[0].shape[1]
    pad = jnp.zeros((width - len(rows), width), F32)
    return jnp.transpose(jnp.concatenate(rows + [pad], axis=0))[0:chans]


def column(cols, k, width):
    return jnp.broadcast_to(cols[:, k : k + 1], (cols.shape[0], width))


def widened(row, width):
    return jnp.concatenate([row, jnp.zeros((1, width - row.shape[1]), F32)], axis=1)


def silu_kernel(
    stat_ref, conv_ref, cot_ref, mask_ref, gain_ref, bias_ref, act_ref, dpre_ref, par_ref, sum_ref, maskf, tmp
):
    batch, chans, flat = conv_ref.shape
    high, width = mask_ref.shape
    maskf[...] = flags(mask_ref)
    stat = stat_ref[:, 0, :]
    n = stat_ref[:, 1, :]
    count = jnp.maximum(jnp.sum(n, axis=0, keepdims=True), 1.0)
    both = jnp.sum(stat, axis=0, keepdims=True)
    mean = both / count
    off = stat / jnp.maximum(n, 1.0) - mean
    between = jnp.sum(n * off * off, axis=0, keepdims=True)
    var = (rolled(both, chans, width) + between) / count
    inv = lax.rsqrt(var + EPS)
    gain = widened(gain_ref[...], width)
    bias = widened(bias_ref[...], width)
    cols = columns([mean, inv, gain, 0.5 * gain * inv, 0.5 * bias, count], chans)
    par_ref[...] = cols
    mean, slope, shift = (column(cols, k, width) for k in (0, 3, 4))
    sums = (jnp.zeros((chans, width), F32), jnp.zeros((chans, width), F32))
    for b in range(batch):

        def row(h, sums, b=b):
            at = row_lanes(h, width)
            dev = conv_ref[b, :, at] - mean
            half = slope * dev + shift
            t = jnp.tanh(half)
            s = 0.5 + 0.5 * t
            act = half + half * t
            tmp[channel_rows(tmp, b, h, chans, high), :] = act * maskf[pl.ds(h, 1), :]
            dpre = cot_ref[b, :, at].astype(F32) * (s + act * (0.5 - 0.5 * t))
            dpre_ref[b, :, at] = dpre
            return sums[0] + dpre, sums[1] + dpre * dev

        sums = lax.fori_loop(0, high, row, sums, unroll=4)
    total = lanes_sum(sums[0], sums[1] * column(cols, 1, width))
    sum_ref[...] = jnp.broadcast_to(total[None], sum_ref.shape)
    for b in range(batch):
        pack_rows(tmp.at[b * chans * (high + 1) : (b + 1) * chans * (high + 1)], act_ref.at[b], chans, high)


def grad_kernel(
    sum_ref, conv_ref, dpre_ref, par_ref, pad_ref, stack_ref, mask_ref,
    d_ref, top_ref, bot_ref, side_ref, out_ref, bg_ref, gg_ref, maskf, acc, da, db, wg_ref,
):
    batch, chans, flat = conv_ref.shape
    high, width = mask_ref.shape
    lane = lane_of(chans, width)
    maskf[...] = flags(mask_ref)
    both = jnp.sum(sum_ref[:, 0, :], axis=0, keepdims=True)
    bg_ref[...] = both[:, 0:chans]
    gg_ref[...] = both[:, chans : 2 * chans]
    cols = par_ref[...]
    mean, inv, gain, count = (column(cols, k, width) for k in (0, 1, 2, 5))
    sums = columns([both], 2 * chans)
    scale = gain * inv
    first = scale * column(sums[0:chans], 0, width) / count
    second = scale * inv * column(sums[chans:], 0, width) / count
    acc[...] = jnp.zeros_like(acc)
    contract = (((1,), (1,)), ((), ()))
    per = high // GROUP
    steps = batch * per

    def place(k):
        return lax.div(k, per), lax.rem(k, per) * GROUP

    def build(k, buf, side):
        b, j = place(k)
        for r in range(GROUP):
            h = j + r
            at = row_lanes(h, width)
            dev = conv_ref[b, :, at] - mean
            d = (maskf[pl.ds(h, 1), :] * (scale * dpre_ref[b, :, at] - first - dev * second)).astype(BF16)
            d_ref[b, :, at] = d
            v = d.astype(F32)
            side = packed(side, v, b * high + h, lane)
            cut = slice(r * width, (r + 1) * width)
            buf[0:chans, cut] = jnp.where(lane == width - 1, 0.0, rolled(v, -1, width)).astype(BF16)
            buf[chans : 2 * chans, cut] = d
            buf[2 * chans :, cut] = jnp.where(lane == 0, 0.0, rolled(v, 1, width)).astype(BF16)
        return side

    def product(k, buf):
        b, j = place(k)
        rhs = buf[...]
        return lax.dot_general(taps(pad_ref, b, j, width, GROUP), rhs, contract, preferred_element_type=F32)

    def pair(p, side):
        k = 2 * p
        gain = product(k, da)
        side = build(k + 1, db, side)
        acc[...] += gain
        gain = product(k + 1, db)
        side = build(jnp.minimum(k + 2, steps - 1), da, side)
        acc[...] += gain
        return side

    side = build(0, da, jnp.zeros((chans, width), F32))
    side = lax.fori_loop(0, steps // 2, pair, side)
    for b in range(batch):
        top_ref[b] = d_ref[b, :, 0:width]
        bot_ref[b] = d_ref[b, :, (high - 1) * width : high * width]
    side_ref[...] = side.astype(BF16)
    even = lax.rem(lane, 2) == 0
    zero = jnp.zeros((chans, width), F32)
    rim = jnp.concatenate([jnp.where(even, side, 0.0), zero, jnp.where(even, 0.0, side)], axis=0)
    full = acc[...] + lax.dot_general(
        stack_ref[...], rim.astype(BF16), contract, preferred_element_type=F32
    )
    half = 3 * chans // 2
    wg_ref[0 : 3 * chans, :] = full[:, 0 : 2 * chans]
    wg_ref[3 * chans : 3 * chans + half, :] = jnp.concatenate(
        [full[0:half, 2 * chans :], full[half:, 2 * chans :]], axis=1
    )
    share = out_ref.shape[1]
    if wg_ref.shape[0] > 3 * chans + half:
        wg_ref[3 * chans + half :, :] = jnp.zeros((wg_ref.shape[0] - 3 * chans - half, width), F32)
    for p in range(out_ref.shape[0]):
        out_ref[p] = wg_ref[p * share : (p + 1) * share, :]


def total_kernel(x_ref, out_ref):
    total = jnp.sum(x_ref[...], axis=0, keepdims=True)
    out_ref[...] = jnp.broadcast_to(total, out_ref.shape)


def unpack_kernel(chans, x_ref, out_ref, wg_ref):
    half = 3 * chans // 2
    share = x_ref.shape[1]
    for p in range(x_ref.shape[0]):
        wg_ref[p * share : (p + 1) * share, :] = x_ref[p]
    for ky in range(3):
        for kx in range(2):
            out_ref[ky, kx] = wg_ref[ky * chans : (ky + 1) * chans, kx * chans : (kx + 1) * chans]
    tail = jnp.concatenate(
        [
            wg_ref[3 * chans : 3 * chans + half, 0:chans],
            wg_ref[3 * chans : 3 * chans + half, chans : 2 * chans],
        ],
        axis=0,
    )
    for ky in range(3):
        out_ref[ky, 2] = tail[ky * chans : (ky + 1) * chans]


def back_kernel(plane, d_ref, above_ref, below_ref, edge_ref, w_ref, mask_ref, *rest):
    out_ref, pad_ref, maskf, tmp, *bufs, tile, sem = rest[-10:]
    batch, chans, flat = d_ref.shape
    high, width = mask_ref.shape
    lane = lane_of(chans, width)
    maskf[...] = flags(mask_ref)
    fill_padded(pad_ref, d_ref, above_ref, below_ref, width, [plane])
    fix = edge_fix(w_ref, edge_stack(edge_ref, above_ref, below_ref, high, batch), lane)

    def post(b, h, value, carry):
        tmp[channel_rows(tmp, 0, h, chans, high), :] = value * maskf[pl.ds(h, 1), :]
        return carry

    conv_loop(pad_ref, w_ref, bufs, fix, plane, high, lane, post, 0)
    pack_rows(tmp, tile, chans, high)
    copy = pltpu.make_async_copy(tile, out_ref.at[plane], sem)
    copy.start()
    copy.wait()


def neighbours(axis, ring):
    n = lax.axis_size(axis)
    even = [(i, i ^ 1) for i in range(n)]
    odd = [(i, (i + 1) % n if i % 2 else (i - 1) % n) for i in range(n)]
    if not ring:
        odd = [pair for pair in odd if pair not in ((0, n - 1), (n - 1, 0))]
    return even, odd


def lon_swap(side):
    n = lax.axis_size("lon")
    if n % 2:
        from_left = lax.ppermute(side, "lon", [(i, (i + 1) % n) for i in range(n)])
        from_right = lax.ppermute(side, "lon", [((i + 1) % n, i) for i in range(n)])
        return from_left, from_right
    even, odd = neighbours("lon", True)
    first = lax.ppermute(side, "lon", even)
    second = lax.ppermute(side, "lon", odd)
    flag = lax.axis_index("lon") % 2 == 1
    return jnp.where(flag, first, second), jnp.where(flag, second, first)


def lat_swap(up, dn):
    n = lax.axis_size("lat")
    if n % 2:
        above = lax.ppermute(dn, "lat", [(i, i + 1) for i in range(n - 1)])
        below = lax.ppermute(up, "lat", [(i + 1, i) for i in range(n - 1)])
        return above, below
    even, odd = neighbours("lat", False)
    flag = lax.axis_index("lat") % 2 == 1
    second = lax.ppermute(jnp.where(flag, dn, up), "lat", odd)
    first = lax.ppermute(jnp.where(flag, up, dn), "lat", even)
    return jnp.where(flag, first, second), jnp.where(flag, second, first)


def with_corners(top, bot, sides, high):
    batch, chans, width = top.shape
    shapes = (
        jax.ShapeDtypeStruct((chans, width), BF16),
        jax.ShapeDtypeStruct((batch + 1, chans, width), BF16),
        jax.ShapeDtypeStruct((batch + 1, chans, width), BF16),
    )
    return call(functools.partial(corner_kernel, high, batch), shapes, [], 0, 200_000, top, bot, *sides)


def on_device(state, land_mask, conv_weight, norm_gain, batchnorm_bias, cotangent):
    batch, chans, high, width = state.shape
    flat = high * width
    axes = ("lat", "lon")
    devices = lax.axis_size(axes)
    S = jax.ShapeDtypeStruct
    mat = 2 * batch * flat * 9 * chans * chans
    size = batch * chans * flat * 2
    tmp = pltpu.VMEM((batch * chans * (high + 1), width), F32)
    maskf = pltpu.VMEM((high, width), F32)
    products = [pltpu.VMEM((3 * chans, STEP * width), F32)] * 4
    plane = S((batch, chans, flat), BF16)
    wide = S((batch, chans, flat), F32)
    rows = S((batch, chans, width), BF16)
    cols = S((chans, width), BF16)
    square = S((3 * chans, 3 * chans), BF16)
    incoming = [
        tmp,
        pltpu.VMEM(state.shape, BF16),
        pltpu.VMEM(land_mask.shape, jnp.int32),
        pltpu.SemaphoreType.DMA((batch * chans // CHUNK,)),
        pltpu.SemaphoreType.DMA,
    ]
    weights = [pltpu.VMEM(conv_weight.shape, BF16), pltpu.SemaphoreType.DMA]
    xm, top, bot, side = call(
        gather_kernel, (plane, rows, rows, cols), incoming, 0, 2 * size, state, land_mask, fetch=True
    )
    cot, w_fwd, w_back = call(
        relay_kernel, (plane, square, square), incoming + weights, 0, 2 * size,
        cotangent, land_mask, conv_weight, fetch=True,
    )
    edge, up, dn = with_corners(top, bot, lon_swap(side), high)
    above, below = lat_swap(up, dn)
    conv, padded, stack, stat = call(
        conv_kernel,
        (
            wide,
            S((batch, chans, flat + 2 * width), BF16),
            S((3 * chans, width), BF16),
            S((devices, 2, 2 * chans), F32),
        ),
        [maskf] + products,
        4 * mat,
        4 * size,
        xm, above, below, edge, w_fwd, land_mask,
    )
    stats = lax.all_to_all(stat, axes, 0, 0)
    activated, dpre, par, sums = call(
        silu_kernel,
        (S(state.shape, BF16), wide, S((chans, width), F32), S((devices, 1, 2 * chans), F32)),
        [maskf, tmp],
        20 * size,
        6 * size,
        stats, conv, cot, land_mask, norm_gain[None], batchnorm_bias[None],
    )
    sums = lax.all_to_all(sums, axes, 0, 0)
    stacked = pltpu.VMEM((3 * chans, GROUP * width), BF16)
    share = -(-9 * chans * chans // (width * devices))
    flatg = pltpu.VMEM((share * devices, width), F32)
    dmap, top, bot, side, wg, bg, gg = call(
        grad_kernel,
        (
            plane, rows, rows, cols,
            S((devices, share, width), F32), S((1, chans), F32), S((1, chans), F32),
        ),
        [maskf, pltpu.VMEM((3 * chans, 3 * chans), F32), stacked, stacked, flatg],
        4 * mat,
        6 * size,
        sums, conv, dpre, par, padded, stack, land_mask,
    )

    parts = lax.all_to_all(wg, axes, 0, 0)
    edge, up, dn = with_corners(top, bot, lon_swap(side), high)
    above, below = lat_swap(up, dn)
    parts, above, below, edge = lax.optimization_barrier((parts, above, below, edge))
    shares = call(total_kernel, S((devices, share, width), F32), [], 0, 600_000, parts)
    wg = lax.all_to_all(shares, axes, 0, 0)

    def backward(b, earlier):
        kept = {} if earlier is None else {"input_output_aliases": {6: 0}}
        whole = pl.BlockSpec(memory_space=pltpu.VMEM)
        far = pl.BlockSpec(memory_space=pl.ANY)
        extra = [] if earlier is None else [earlier]
        return pl.pallas_call(
            functools.partial(back_kernel, b),
            out_shape=S(state.shape, BF16),
            in_specs=[whole] * 6 + [far] * len(extra),
            out_specs=far,
            scratch_shapes=[
                pltpu.VMEM((1, chans, flat + 2 * width), BF16),
                maskf,
                pltpu.VMEM((chans * (high + 1), width), F32),
            ]
            + products
            + [pltpu.VMEM((chans, high, width), BF16), pltpu.SemaphoreType.DMA],
            compiler_params=pltpu.CompilerParams(vmem_limit_bytes=24 << 20),
            cost_estimate=pl.CostEstimate(flops=2 * mat, bytes_accessed=2 * size, transcendentals=0),
            **kept,
        )(dmap, above, below, edge, w_back, land_mask, *extra)

    state_grad = None
    for b in range(batch):
        state_grad = backward(b, state_grad)
    weight_grad = call(
        functools.partial(unpack_kernel, chans), S((3, 3, chans, chans), F32), [flatg], 0, 500_000, wg
    )
    return (activated, state_grad, weight_grad, gg[0], bg[0])


def solution(mesh):
    return jax.shard_map(
        on_device,
        mesh=mesh,
        in_specs=(
            P(None, None, "lat", "lon"),
            P("lat", "lon"),
            P(),
            P(),
            P(),
            P(None, None, "lat", "lon"),
        ),
        out_specs=(P(None, None, "lat", "lon"), P(None, None, "lat", "lon"), P(), P(), P()),
        check_vma=False,
    )
```

```python
import functools

import jax
import jax.numpy as jnp
from jax import lax
from jax.experimental import pallas as pl
from jax.experimental.pallas import tpu as pltpu
from jax.sharding import PartitionSpec as P


F32 = jnp.float32
BF16 = jnp.bfloat16
STEP = 2
GROUP = 4
EPS = 1e-05


def lane_of(rows, width):
    return lax.broadcasted_iota(jnp.int32, (rows, width), 1)


def rolled(value, shift, width):
    return pltpu.roll(value, lax.rem(shift + 4 * width, width), 1)


def any_lane(lane, picks):
    hit = lane == picks[0]
    for p in picks[1:]:
        hit = jnp.logical_or(hit, lane == p)
    return hit


def call(kernel, out_shape, scratch, flops, nbytes, *args):
    return pl.pallas_call(
        kernel,
        out_shape=out_shape,
        in_specs=[pl.BlockSpec(memory_space=pltpu.VMEM)] * len(args),
        scratch_shapes=scratch,
        compiler_params=pltpu.CompilerParams(vmem_limit_bytes=24 << 20),
        cost_estimate=pl.CostEstimate(flops=flops, bytes_accessed=nbytes, transcendentals=0),
    )(*args)


def row_lanes(h, width, count=1):
    return pl.ds(pl.multiple_of(h * width, width), count * width)


def spread_rows(src_ref, tmp, mask):
    batch, chans, high, _ = src_ref.shape
    for b in range(batch):
        for c in range(chans):
            at = (b * chans + c) * (high + 1)
            tmp[at : at + high, :] = src_ref[b, c].astype(F32) * mask


def channel_rows(b, h, chans, high):
    return pl.ds(b * chans * (high + 1) + h, chans, stride=high + 1)


def pack_rows(tmp, out, chans, high):
    for c in range(chans):
        at = c * (high + 1)
        out[c] = tmp[at : at + high, :].astype(BF16)


def packed(old, v, i, lane):
    width = lane.shape[1]
    here = jnp.logical_or(lane == 2 * i, lane == lax.rem(2 * i - 1 + width, width))
    return jnp.where(here, rolled(v, 2 * i, width), old)


def gather_kernel(x_ref, mask_ref, xm_ref, top_ref, bot_ref, side_ref, maskf, tmp):
    batch, chans, high, width = x_ref.shape
    maskf[...] = mask_ref[...].astype(F32)
    spread_rows(x_ref, tmp, maskf[...])
    lane = lane_of(chans, width)
    side = jnp.zeros((chans, width), F32)
    for b in range(batch):

        def row(h, side, b=b):
            v = tmp[channel_rows(b, h, chans, high), :]
            xm_ref[b, :, row_lanes(h, width)] = v.astype(BF16)
            return packed(side, v, b * high + h, lane)

        side = lax.fori_loop(0, high, row, side, unroll=8)
        top_ref[b] = xm_ref[b, :, 0:width]
        bot_ref[b] = xm_ref[b, :, (high - 1) * width : high * width]
    side_ref[...] = side.astype(BF16)


def relay_kernel(x_ref, maskf, w_ref, out_ref, fwd_ref, back_ref, tmp):
    batch, chans, high, width = x_ref.shape
    spread_rows(x_ref, tmp, maskf[...])
    for kx in range(3):
        part = jnp.concatenate([w_ref[ky, kx].astype(F32) for ky in range(3)], axis=0)
        fwd_ref[kx * chans : (kx + 1) * chans, :] = jnp.transpose(part).astype(BF16)
        part = [w_ref[2 - ky, 2 - kx].astype(F32) for ky in range(3)]
        back_ref[kx * chans : (kx + 1) * chans, :] = jnp.concatenate(part, axis=1).astype(BF16)
    for b in range(batch):

        def row(h, carry, b=b):
            out_ref[b, :, row_lanes(h, width)] = tmp[channel_rows(b, h, chans, high), :].astype(BF16)
            return carry

        lax.fori_loop(0, high, row, 0, unroll=8)


def corners(high, batch, width):
    first = [(2 * b * high + d) % width for b in range(batch) for d in (0, -1)]
    return first, [(p + 2 * (high - 1)) % width for p in first]


def corner_kernel(high, batch, top_ref, bot_ref, fl_ref, fr_ref, edge_ref, up_ref, dn_ref):
    chans, width = fl_ref.shape
    lane = lane_of(chans, width)
    even = lax.rem(lane, 2) == 0
    edge = jnp.where(
        even, rolled(fl_ref[...].astype(F32), 1, width), rolled(fr_ref[...].astype(F32), -1, width)
    )
    first, last = corners(high, batch, width)
    far = 2 * (high - 1)
    edge_ref[...] = edge.astype(BF16)
    up = jnp.where(any_lane(lane, last), rolled(edge, far, width), 0.0)
    dn = jnp.where(any_lane(lane, first), rolled(edge, -far, width), 0.0)
    for b in range(batch):
        up_ref[b] = top_ref[b]
        dn_ref[b] = bot_ref[b]
    up_ref[batch] = up.astype(BF16)
    dn_ref[batch] = dn.astype(BF16)


def edge_stack(edge_ref, above_ref, below_ref, high, batch):
    chans, width = edge_ref.shape
    lane = lane_of(chans, width)
    edge = edge_ref[...].astype(F32)
    first, last = corners(high, batch, width)
    top = jnp.where(any_lane(lane, first), above_ref[batch].astype(F32), rolled(edge, 2, width))
    bottom = jnp.where(any_lane(lane, last), below_ref[batch].astype(F32), rolled(edge, -2, width))
    return jnp.concatenate([top, edge, bottom], axis=0).astype(BF16)


def fill_padded(pad_ref, x_ref, above_ref, below_ref, width, planes):
    flat = x_ref.shape[2]
    for to, b in enumerate(planes):
        pad_ref[to, :, 0:width] = above_ref[b]
        pad_ref[to, :, width : width + flat] = x_ref[b]
        pad_ref[to, :, width + flat :] = below_ref[b]


def taps(pad_ref, b, j, width, count):
    return jnp.concatenate([pad_ref[b, :, row_lanes(j + ky, width, count)] for ky in range(3)], axis=0)


def edge_fix(w_ref, stack, lane):
    g = jnp.dot(w_ref[...], stack, preferred_element_type=F32)
    c = g.shape[0] // 3
    return jnp.where(lax.rem(lane, 2) == 0, g[0:c], g[2 * c :])


def conv_loop(pad_ref, w_ref, bufs, fix, first, high, lane, post, carry):
    planes = pad_ref.shape[0]
    chans, width = lane.shape
    per = high // STEP
    steps = planes * per

    def product(k, buf):
        k = jnp.minimum(k, steps - 1)
        b, j = lax.div(k, per), lax.rem(k, per) * STEP
        buf[...] = jnp.dot(w_ref[...], taps(pad_ref, b, j, width, STEP), preferred_element_type=F32)

    def finish(k, buf, carry):
        b, j = lax.div(k, per), lax.rem(k, per) * STEP
        for r in range(STEP):
            cut = slice(r * width, (r + 1) * width)
            g = rolled(fix, -2 * ((first + b) * high + j + r), width)
            left = jnp.where(lane == 0, g, rolled(buf[0:chans, cut], 1, width))
            right = jnp.where(lane == width - 1, g, rolled(buf[2 * chans :, cut], -1, width))
            carry = post(b, j + r, left + buf[chans : 2 * chans, cut] + right, carry)
        return carry

    def four(p, carry):
        k = 4 * p
        product(k + 2, bufs[2])
        product(k + 3, bufs[3])
        carry = finish(k, bufs[0], carry)
        carry = finish(k + 1, bufs[1], carry)
        product(k + 4, bufs[0])
        product(k + 5, bufs[1])
        carry = finish(k + 2, bufs[2], carry)
        return finish(k + 3, bufs[3], carry)

    product(0, bufs[0])
    product(1, bufs[1])
    return lax.fori_loop(0, steps // 4, four, carry)


def lanes_sum(first, second):
    both = jnp.concatenate([first, second], axis=0)
    return jnp.sum(jnp.transpose(both), axis=0, keepdims=True)


def conv_kernel(
    x_ref, above_ref, below_ref, edge_ref, w_ref, maskf,
    conv_ref, pad_ref, stack_ref, stat_ref, *bufs,
):
    batch, chans, _ = x_ref.shape
    high, width = maskf.shape
    lane = lane_of(chans, width)
    fill_padded(pad_ref, x_ref, above_ref, below_ref, width, range(batch))
    stack = edge_stack(edge_ref, above_ref, below_ref, high, batch)
    stack_ref[...] = stack
    fix = edge_fix(w_ref, stack, lane)

    def post(b, h, value, total):
        conv_ref[b, :, row_lanes(h, width)] = value
        return total + value * maskf[pl.ds(h, 1), :]

    zero = jnp.zeros((chans, width), F32)
    total = conv_loop(pad_ref, w_ref, bufs, fix, 0, high, lane, post, zero)
    n = batch * jnp.sum(maskf[...])
    mean = jnp.sum(total, axis=1, keepdims=True) / jnp.maximum(n, 1.0)
    mean = jnp.broadcast_to(mean, (chans, width))
    spread = zero
    for b in range(batch):

        def step(h, spread, b=b):
            dev = conv_ref[b, :, row_lanes(h, width)] - mean
            return spread + dev * dev * maskf[pl.ds(h, 1), :]

        spread = lax.fori_loop(0, high, step, spread, unroll=8)
    copies = stat_ref.shape[0]
    stat_ref[:, 0:1, :] = jnp.broadcast_to(lanes_sum(total, spread)[None], (copies, 1, 2 * chans))
    stat_ref[:, 1:2, :] = jnp.full((copies, 1, 2 * chans), n, F32)


def columns(rows, chans):
    width = rows[0].shape[1]
    pad = jnp.zeros((width - len(rows), width), F32)
    return jnp.transpose(jnp.concatenate(rows + [pad], axis=0))[0:chans]


def column(cols, k, width):
    return jnp.broadcast_to(cols[:, k : k + 1], (cols.shape[0], width))


def widened(row, width):
    return jnp.concatenate([row, jnp.zeros((1, width - row.shape[1]), F32)], axis=1)


def silu_kernel(
    stat_ref, conv_ref, cot_ref, maskf, gain_ref, bias_ref, act_ref, dpre_ref, par_ref, sum_ref, tmp
):
    batch, chans, _ = conv_ref.shape
    high, width = maskf.shape
    stat = stat_ref[:, 0, :]
    n = stat_ref[:, 1, :]
    count = jnp.maximum(jnp.sum(n, axis=0, keepdims=True), 1.0)
    both = jnp.sum(stat, axis=0, keepdims=True)
    mean = both / count
    off = stat / jnp.maximum(n, 1.0) - mean
    between = jnp.sum(n * off * off, axis=0, keepdims=True)
    var = (rolled(both, chans, width) + between) / count
    inv = lax.rsqrt(var + EPS)
    gain = widened(gain_ref[...], width)
    bias = widened(bias_ref[...], width)
    cols = columns([mean, inv, gain, 0.5 * gain * inv, 0.5 * bias, count], chans)
    par_ref[...] = cols
    mean, slope, shift = (column(cols, k, width) for k in (0, 3, 4))
    sums = (jnp.zeros((chans, width), F32), jnp.zeros((chans, width), F32))
    for b in range(batch):

        def row(h, sums, b=b):
            at = row_lanes(h, width)
            dev = conv_ref[b, :, at] - mean
            half = slope * dev + shift
            t = jnp.tanh(half)
            s = 0.5 + 0.5 * t
            act = half + half * t
            tmp[channel_rows(b, h, chans, high), :] = act * maskf[pl.ds(h, 1), :]
            dpre = cot_ref[b, :, at].astype(F32) * (s + act * (0.5 - 0.5 * t))
            dpre_ref[b, :, at] = dpre
            return sums[0] + dpre, sums[1] + dpre * dev

        sums = lax.fori_loop(0, high, row, sums, unroll=4)
    total = lanes_sum(sums[0], sums[1] * column(cols, 1, width))
    sum_ref[...] = jnp.broadcast_to(total[None], sum_ref.shape)
    for b in range(batch):
        pack_rows(tmp.at[b * chans * (high + 1) : (b + 1) * chans * (high + 1)], act_ref.at[b], chans, high)


def grad_kernel(
    sum_ref, conv_ref, dpre_ref, par_ref, pad_ref, stack_ref, maskf,
    d_ref, top_ref, bot_ref, side_ref, out_ref, bg_ref, gg_ref, acc, da, db, wg_ref,
):
    batch, chans, _ = conv_ref.shape
    high, width = maskf.shape
    lane = lane_of(chans, width)
    both = jnp.sum(sum_ref[:, 0, :], axis=0, keepdims=True)
    bg_ref[...] = both[:, 0:chans]
    gg_ref[...] = both[:, chans : 2 * chans]
    cols = par_ref[...]
    mean, inv, gain, count = (column(cols, k, width) for k in (0, 1, 2, 5))
    sums = columns([both], 2 * chans)
    scale = gain * inv
    first = scale * column(sums[0:chans], 0, width) / count
    second = scale * inv * column(sums[chans:], 0, width) / count
    acc[...] = jnp.zeros_like(acc)
    contract = (((1,), (1,)), ((), ()))
    per = high // GROUP
    steps = batch * per

    def place(k):
        return lax.div(k, per), lax.rem(k, per) * GROUP

    def build(k, buf, side):
        b, j = place(k)
        for r in range(GROUP):
            h = j + r
            at = row_lanes(h, width)
            dev = conv_ref[b, :, at] - mean
            d = (maskf[pl.ds(h, 1), :] * (scale * dpre_ref[b, :, at] - first - dev * second)).astype(BF16)
            d_ref[b, :, at] = d
            v = d.astype(F32)
            side = packed(side, v, b * high + h, lane)
            cut = slice(r * width, (r + 1) * width)
            buf[0:chans, cut] = jnp.where(lane == width - 1, 0.0, rolled(v, -1, width)).astype(BF16)
            buf[chans : 2 * chans, cut] = d
            buf[2 * chans :, cut] = jnp.where(lane == 0, 0.0, rolled(v, 1, width)).astype(BF16)
        return side

    def product(k, buf):
        b, j = place(k)
        rhs = buf[...]
        return lax.dot_general(taps(pad_ref, b, j, width, GROUP), rhs, contract, preferred_element_type=F32)

    def pair(p, side):
        k = 2 * p
        gain = product(k, da)
        side = build(k + 1, db, side)
        acc[...] += gain
        gain = product(k + 1, db)
        side = build(jnp.minimum(k + 2, steps - 1), da, side)
        acc[...] += gain
        return side

    side = build(0, da, jnp.zeros((chans, width), F32))
    side = lax.fori_loop(0, steps // 2, pair, side)
    for b in range(batch):
        top_ref[b] = d_ref[b, :, 0:width]
        bot_ref[b] = d_ref[b, :, (high - 1) * width : high * width]
    side_ref[...] = side.astype(BF16)
    even = lax.rem(lane, 2) == 0
    zero = jnp.zeros((chans, width), F32)
    rim = jnp.concatenate([jnp.where(even, side, 0.0), zero, jnp.where(even, 0.0, side)], axis=0)
    full = acc[...] + lax.dot_general(
        stack_ref[...], rim.astype(BF16), contract, preferred_element_type=F32
    )
    half = 3 * chans // 2
    wg_ref[0 : 3 * chans, :] = full[:, 0 : 2 * chans]
    wg_ref[3 * chans : 3 * chans + half, :] = jnp.concatenate(
        [full[0:half, 2 * chans :], full[half:, 2 * chans :]], axis=1
    )
    if wg_ref.shape[0] > 3 * chans + half:
        wg_ref[3 * chans + half :, :] = jnp.zeros((wg_ref.shape[0] - 3 * chans - half, width), F32)
    share = out_ref.shape[2] // width
    for p in range(out_ref.shape[0]):
        for r in range(share):
            out_ref[p, :, r * width : (r + 1) * width] = wg_ref[p * share + r : p * share + r + 1, :]


def total_kernel(x_ref, out_ref):
    total = jnp.sum(x_ref[...], axis=0, keepdims=True)
    out_ref[...] = jnp.broadcast_to(total, out_ref.shape)


def unpack_kernel(chans, x_ref, out_ref, wg_ref):
    half = 3 * chans // 2
    width = wg_ref.shape[1]
    share = x_ref.shape[2] // width
    for p in range(x_ref.shape[0]):
        for r in range(share):
            wg_ref[p * share + r : p * share + r + 1, :] = x_ref[p, :, r * width : (r + 1) * width]
    for ky in range(3):
        for kx in range(2):
            out_ref[ky, kx] = wg_ref[ky * chans : (ky + 1) * chans, kx * chans : (kx + 1) * chans]
    tail = jnp.concatenate(
        [
            wg_ref[3 * chans : 3 * chans + half, 0:chans],
            wg_ref[3 * chans : 3 * chans + half, chans : 2 * chans],
        ],
        axis=0,
    )
    for ky in range(3):
        out_ref[ky, 2] = tail[ky * chans : (ky + 1) * chans]


def back_kernel(plane, d_ref, above_ref, below_ref, edge_ref, w_ref, maskf, *rest):
    out_ref, pad_ref, tmp, *bufs, tile, sem = rest[-9:]
    batch, chans, _ = d_ref.shape
    high, width = maskf.shape
    lane = lane_of(chans, width)
    fill_padded(pad_ref, d_ref, above_ref, below_ref, width, [plane])
    fix = edge_fix(w_ref, edge_stack(edge_ref, above_ref, below_ref, high, batch), lane)

    def post(b, h, value, carry):
        tmp[channel_rows(0, h, chans, high), :] = value * maskf[pl.ds(h, 1), :]
        return carry

    conv_loop(pad_ref, w_ref, bufs, fix, plane, high, lane, post, 0)
    pack_rows(tmp, tile, chans, high)
    copy = pltpu.make_async_copy(tile, out_ref.at[plane], sem)
    copy.start()
    copy.wait()


def neighbours(axis, ring):
    n = lax.axis_size(axis)
    even = [(i, i ^ 1) for i in range(n)]
    odd = [(i, (i + 1) % n if i % 2 else (i - 1) % n) for i in range(n)]
    if not ring:
        odd = [pair for pair in odd if pair not in ((0, n - 1), (n - 1, 0))]
    return even, odd


def lon_swap(side):
    n = lax.axis_size("lon")
    if n % 2:
        from_left = lax.ppermute(side, "lon", [(i, (i + 1) % n) for i in range(n)])
        from_right = lax.ppermute(side, "lon", [((i + 1) % n, i) for i in range(n)])
        return from_left, from_right
    even, odd = neighbours("lon", True)
    first = lax.ppermute(side, "lon", even)
    second = lax.ppermute(side, "lon", odd)
    flag = lax.axis_index("lon") % 2 == 1
    return jnp.where(flag, first, second), jnp.where(flag, second, first)


def lat_swap(up, dn):
    n = lax.axis_size("lat")
    if n % 2:
        above = lax.ppermute(dn, "lat", [(i, i + 1) for i in range(n - 1)])
        below = lax.ppermute(up, "lat", [(i + 1, i) for i in range(n - 1)])
        return above, below
    even, odd = neighbours("lat", False)
    flag = lax.axis_index("lat") % 2 == 1
    second = lax.ppermute(jnp.where(flag, dn, up), "lat", odd)
    first = lax.ppermute(jnp.where(flag, up, dn), "lat", even)
    return jnp.where(flag, first, second), jnp.where(flag, second, first)


def with_corners(top, bot, sides, high):
    batch, chans, width = top.shape
    shapes = (
        jax.ShapeDtypeStruct((chans, width), BF16),
        jax.ShapeDtypeStruct((batch + 1, chans, width), BF16),
        jax.ShapeDtypeStruct((batch + 1, chans, width), BF16),
    )
    return call(functools.partial(corner_kernel, high, batch), shapes, [], 0, 200_000, top, bot, *sides)


def on_device(state, land_mask, conv_weight, norm_gain, batchnorm_bias, cotangent):
    batch, chans, high, width = state.shape
    flat = high * width
    axes = ("lat", "lon")
    devices = lax.axis_size(axes)
    S = jax.ShapeDtypeStruct
    mat = 2 * batch * flat * 9 * chans * chans
    size = batch * chans * flat * 2
    tmp = pltpu.VMEM((batch * chans * (high + 1), width), F32)
    products = [pltpu.VMEM((3 * chans, STEP * width), F32)] * 4
    plane = S((batch, chans, flat), BF16)
    wide = S((batch, chans, flat), F32)
    rows = S((batch, chans, width), BF16)
    cols = S((chans, width), BF16)
    square = S((3 * chans, 3 * chans), BF16)
    xm, top, bot, side, flag = call(
        gather_kernel, (plane, rows, rows, cols, S((high, width), F32)), [tmp], 0, 2 * size, state, land_mask
    )
    cot, w_fwd, w_back = call(
        relay_kernel, (plane, square, square), [tmp], 0, 2 * size, cotangent, flag, conv_weight
    )
    sides = lon_swap(side)
    sides, cot, w_fwd, w_back = lax.optimization_barrier((sides, cot, w_fwd, w_back))
    edge, up, dn = with_corners(top, bot, sides, high)
    above, below = lat_swap(up, dn)
    conv, padded, stack, stat = call(
        conv_kernel,
        (
            wide,
            S((batch, chans, flat + 2 * width), BF16),
            S((3 * chans, width), BF16),
            S((devices, 2, 2 * chans), F32),
        ),
        products,
        4 * mat,
        4 * size,
        xm, above, below, edge, w_fwd, flag,
    )
    stats = lax.all_to_all(stat, axes, 0, 0)
    activated, dpre, par, sums = call(
        silu_kernel,
        (S(state.shape, BF16), wide, S((chans, width), F32), S((devices, 1, 2 * chans), F32)),
        [tmp],
        20 * size,
        6 * size,
        stats, conv, cot, flag, norm_gain[None], batchnorm_bias[None],
    )
    sums = lax.all_to_all(sums, axes, 0, 0)
    stacked = pltpu.VMEM((3 * chans, GROUP * width), BF16)
    share = -(-9 * chans * chans // (width * devices))
    flatg = pltpu.VMEM((share * devices, width), F32)
    dmap, top, bot, side, wg, bg, gg = call(
        grad_kernel,
        (
            plane, rows, rows, cols,
            S((devices, 1, share * width), F32), S((1, chans), F32), S((1, chans), F32),
        ),
        [pltpu.VMEM((3 * chans, 3 * chans), F32), stacked, stacked, flatg],
        4 * mat,
        6 * size,
        sums, conv, dpre, par, padded, stack, flag,
    )

    parts = lax.all_to_all(wg, axes, 0, 0)
    edge, up, dn = with_corners(top, bot, lon_swap(side), high)
    above, below = lat_swap(up, dn)
    parts, above, below, edge = lax.optimization_barrier((parts, above, below, edge))
    shares = call(total_kernel, S((devices, 1, share * width), F32), [], 0, 600_000, parts)
    wg = lax.all_to_all(shares, axes, 0, 0)

    def backward(b, earlier):
        kept = {} if earlier is None else {"input_output_aliases": {6: 0}}
        whole = pl.BlockSpec(memory_space=pltpu.VMEM)
        far = pl.BlockSpec(memory_space=pl.ANY)
        extra = [] if earlier is None else [earlier]
        return pl.pallas_call(
            functools.partial(back_kernel, b),
            out_shape=S(state.shape, BF16),
            in_specs=[whole] * 6 + [far] * len(extra),
            out_specs=far,
            scratch_shapes=[
                pltpu.VMEM((1, chans, flat + 2 * width), BF16),
                pltpu.VMEM((chans * (high + 1), width), F32),
            ]
            + products
            + [pltpu.VMEM((chans, high, width), BF16), pltpu.SemaphoreType.DMA],
            compiler_params=pltpu.CompilerParams(vmem_limit_bytes=24 << 20),
            cost_estimate=pl.CostEstimate(flops=2 * mat, bytes_accessed=2 * size, transcendentals=0),
            **kept,
        )(dmap, above, below, edge, w_back, flag, *extra)

    state_grad = None
    for b in range(batch):
        state_grad = backward(b, state_grad)
    weight_grad = call(
        functools.partial(unpack_kernel, chans), S((3, 3, chans, chans), F32), [flatg], 0, 500_000, wg
    )
    return (activated, state_grad, weight_grad, gg[0], bg[0])


def solution(mesh):
    return jax.shard_map(
        on_device,
        mesh=mesh,
        in_specs=(
            P(None, None, "lat", "lon"),
            P("lat", "lon"),
            P(),
            P(),
            P(),
            P(None, None, "lat", "lon"),
        ),
        out_specs=(P(None, None, "lat", "lon"), P(None, None, "lat", "lon"), P(), P(), P()),
        check_vma=False,
    )
```

```python
import functools

import jax
import jax.numpy as jnp
from jax import lax
from jax.experimental import pallas as pl
from jax.experimental.pallas import tpu as pltpu
from jax.sharding import PartitionSpec as P


F32 = jnp.float32
BF16 = jnp.bfloat16
STEP = 2
GROUP = 4
EPS = 1e-05


def lane_of(rows, width):
    return lax.broadcasted_iota(jnp.int32, (rows, width), 1)


def rolled(value, shift, width):
    return pltpu.roll(value, lax.rem(shift + 4 * width, width), 1)


def any_lane(lane, picks):
    hit = lane == picks[0]
    for p in picks[1:]:
        hit = jnp.logical_or(hit, lane == p)
    return hit


def call(kernel, out_shape, scratch, flops, nbytes, *args):
    return pl.pallas_call(
        kernel,
        out_shape=out_shape,
        in_specs=[pl.BlockSpec(memory_space=pltpu.VMEM)] * len(args),
        scratch_shapes=scratch,
        compiler_params=pltpu.CompilerParams(vmem_limit_bytes=24 << 20),
        cost_estimate=pl.CostEstimate(flops=flops, bytes_accessed=nbytes, transcendentals=0),
    )(*args)


def row_lanes(h, width, count=1):
    return pl.ds(pl.multiple_of(h * width, width), count * width)


def spread_rows(src_ref, tmp, mask):
    batch, chans, high, _ = src_ref.shape
    for b in range(batch):
        for c in range(chans):
            at = (b * chans + c) * (high + 1)
            tmp[at : at + high, :] = src_ref[b, c].astype(F32) * mask


def channel_rows(b, h, chans, high):
    return pl.ds(b * chans * (high + 1) + h, chans, stride=high + 1)


def pack_rows(tmp, out, chans, high):
    for c in range(chans):
        at = c * (high + 1)
        out[c] = tmp[at : at + high, :].astype(BF16)


def packed(old, v, i, lane):
    width = lane.shape[1]
    here = jnp.logical_or(lane == 2 * i, lane == lax.rem(2 * i - 1 + width, width))
    return jnp.where(here, rolled(v, 2 * i, width), old)


def ends_kernel(x_ref, mask_ref, top_ref, bot_ref, maskf, tmp):
    batch, chans, high, _ = x_ref.shape
    maskf[...] = mask_ref[...].astype(F32)
    for h, out_ref in ((0, top_ref), (high - 1, bot_ref)):
        base = h - h % 16
        for b in range(batch):
            for c in range(chans):
                tile = x_ref[b, c, base : base + 16].astype(F32)
                tmp[c : c + 1, :] = tile[h - base : h - base + 1]
            out_ref[b] = (tmp[...] * maskf[h : h + 1, :]).astype(BF16)


def gather_kernel(x_ref, maskf, xm_ref, side_ref, tmp):
    batch, chans, high, width = x_ref.shape
    spread_rows(x_ref, tmp, maskf[...])
    lane = lane_of(chans, width)
    side = jnp.zeros((chans, width), F32)
    for b in range(batch):

        def row(h, side, b=b):
            v = tmp[channel_rows(b, h, chans, high), :]
            xm_ref[b, :, row_lanes(h, width)] = v.astype(BF16)
            return packed(side, v, b * high + h, lane)

        side = lax.fori_loop(0, high, row, side, unroll=8)
    side_ref[...] = side.astype(BF16)


def relay_kernel(x_ref, maskf, w_ref, out_ref, fwd_ref, back_ref, tmp):
    batch, chans, high, width = x_ref.shape
    spread_rows(x_ref, tmp, maskf[...])
    for kx in range(3):
        part = jnp.concatenate([w_ref[ky, kx].astype(F32) for ky in range(3)], axis=0)
        fwd_ref[kx * chans : (kx + 1) * chans, :] = jnp.transpose(part).astype(BF16)
        part = [w_ref[2 - ky, 2 - kx].astype(F32) for ky in range(3)]
        back_ref[kx * chans : (kx + 1) * chans, :] = jnp.concatenate(part, axis=1).astype(BF16)
    for b in range(batch):

        def row(h, carry, b=b):
            out_ref[b, :, row_lanes(h, width)] = tmp[channel_rows(b, h, chans, high), :].astype(BF16)
            return carry

        lax.fori_loop(0, high, row, 0, unroll=8)


def corners(high, batch, width):
    first = [(2 * b * high + d) % width for b in range(batch) for d in (0, -1)]
    return first, [(p + 2 * (high - 1)) % width for p in first]


def corner_kernel(high, side_ref, above_ref, below_ref, out_ref):
    chans, width = side_ref.shape
    lane = lane_of(chans, width)
    pack = jnp.zeros((chans, width), F32)
    for b in range(above_ref.shape[0]):
        pack = packed(pack, above_ref[b].astype(F32), b * high, lane)
        pack = packed(pack, below_ref[b].astype(F32), b * high + high - 1, lane)
    out_ref[0] = side_ref[...]
    out_ref[1] = pack.astype(BF16)


def pole_kernel(high, batch, top_ref, bot_ref, fl_ref, fr_ref, edge_ref, up_ref, dn_ref):
    chans, width = fl_ref.shape
    lane = lane_of(chans, width)
    even = lax.rem(lane, 2) == 0
    edge = jnp.where(
        even, rolled(fl_ref[...].astype(F32), 1, width), rolled(fr_ref[...].astype(F32), -1, width)
    )
    first, last = corners(high, batch, width)
    far = 2 * (high - 1)
    edge_ref[...] = edge.astype(BF16)
    up = jnp.where(any_lane(lane, last), rolled(edge, far, width), 0.0)
    dn = jnp.where(any_lane(lane, first), rolled(edge, -far, width), 0.0)
    for b in range(batch):
        up_ref[b] = top_ref[b]
        dn_ref[b] = bot_ref[b]
    up_ref[batch] = up.astype(BF16)
    dn_ref[batch] = dn.astype(BF16)


def facing(left, right):
    chans, width = left.shape
    even = lax.rem(lane_of(chans, width), 2) == 0
    return jnp.where(even, rolled(left.astype(F32), 1, width), rolled(right.astype(F32), -1, width))


def edge_stack(edge, above, below, high, batch):
    chans, width = edge.shape
    lane = lane_of(chans, width)
    first, last = corners(high, batch, width)
    top = jnp.where(any_lane(lane, first), above.astype(F32), rolled(edge, 2, width))
    bottom = jnp.where(any_lane(lane, last), below.astype(F32), rolled(edge, -2, width))
    return jnp.concatenate([top, edge, bottom], axis=0).astype(BF16)


def fill_padded(pad_ref, x_ref, above_ref, below_ref, width, planes):
    flat = x_ref.shape[2]
    for to, b in enumerate(planes):
        pad_ref[to, :, 0:width] = above_ref[b]
        pad_ref[to, :, width : width + flat] = x_ref[b]
        pad_ref[to, :, width + flat :] = below_ref[b]


def taps(pad_ref, b, j, width, count):
    return jnp.concatenate([pad_ref[b, :, row_lanes(j + ky, width, count)] for ky in range(3)], axis=0)


def edge_fix(w_ref, stack, lane):
    g = jnp.dot(w_ref[...], stack, preferred_element_type=F32)
    c = g.shape[0] // 3
    return jnp.where(lax.rem(lane, 2) == 0, g[0:c], g[2 * c :])


def conv_loop(pad_ref, w_ref, bufs, fix, first, high, lane, post, carry):
    planes = pad_ref.shape[0]
    chans, width = lane.shape
    per = high // STEP
    steps = planes * per

    def product(k, buf):
        k = jnp.minimum(k, steps - 1)
        b, j = lax.div(k, per), lax.rem(k, per) * STEP
        buf[...] = jnp.dot(w_ref[...], taps(pad_ref, b, j, width, STEP), preferred_element_type=F32)

    def finish(k, buf, carry):
        b, j = lax.div(k, per), lax.rem(k, per) * STEP
        for r in range(STEP):
            cut = slice(r * width, (r + 1) * width)
            g = rolled(fix, -2 * ((first + b) * high + j + r), width)
            left = jnp.where(lane == 0, g, rolled(buf[0:chans, cut], 1, width))
            right = jnp.where(lane == width - 1, g, rolled(buf[2 * chans :, cut], -1, width))
            carry = post(b, j + r, left + buf[chans : 2 * chans, cut] + right, carry)
        return carry

    def four(p, carry):
        k = 4 * p
        product(k + 2, bufs[2])
        product(k + 3, bufs[3])
        carry = finish(k, bufs[0], carry)
        carry = finish(k + 1, bufs[1], carry)
        product(k + 4, bufs[0])
        product(k + 5, bufs[1])
        carry = finish(k + 2, bufs[2], carry)
        return finish(k + 3, bufs[3], carry)

    product(0, bufs[0])
    product(1, bufs[1])
    return lax.fori_loop(0, steps // 4, four, carry)


def lanes_sum(first, second):
    both = jnp.concatenate([first, second], axis=0)
    return jnp.sum(jnp.transpose(both), axis=0, keepdims=True)


def conv_kernel(
    x_ref, above_ref, below_ref, left_ref, right_ref, w_ref, maskf,
    conv_ref, pad_ref, stack_ref, stat_ref, *bufs,
):
    batch, chans, _ = x_ref.shape
    high, width = maskf.shape
    lane = lane_of(chans, width)
    fill_padded(pad_ref, x_ref, above_ref, below_ref, width, range(batch))
    corner = facing(left_ref[1], right_ref[1])
    stack = edge_stack(facing(left_ref[0], right_ref[0]), corner, corner, high, batch)
    stack_ref[...] = stack
    fix = edge_fix(w_ref, stack, lane)

    def post(b, h, value, total):
        conv_ref[b, :, row_lanes(h, width)] = value
        return total + value * maskf[pl.ds(h, 1), :]

    zero = jnp.zeros((chans, width), F32)
    total = conv_loop(pad_ref, w_ref, bufs, fix, 0, high, lane, post, zero)
    n = batch * jnp.sum(maskf[...])
    mean = jnp.sum(total, axis=1, keepdims=True) / jnp.maximum(n, 1.0)
    mean = jnp.broadcast_to(mean, (chans, width))
    spread = zero
    for b in range(batch):

        def step(h, spread, b=b):
            dev = conv_ref[b, :, row_lanes(h, width)] - mean
            return spread + dev * dev * maskf[pl.ds(h, 1), :]

        spread = lax.fori_loop(0, high, step, spread, unroll=8)
    copies = stat_ref.shape[0]
    stat_ref[:, 0:1, :] = jnp.broadcast_to(lanes_sum(total, spread)[None], (copies, 1, 2 * chans))
    stat_ref[:, 1:2, :] = jnp.full((copies, 1, 2 * chans), n, F32)


def columns(rows, chans):
    width = rows[0].shape[1]
    pad = jnp.zeros((width - len(rows), width), F32)
    return jnp.transpose(jnp.concatenate(rows + [pad], axis=0))[0:chans]


def column(cols, k, width):
    return jnp.broadcast_to(cols[:, k : k + 1], (cols.shape[0], width))


def widened(row, width):
    return jnp.concatenate([row, jnp.zeros((1, width - row.shape[1]), F32)], axis=1)


def silu_kernel(
    stat_ref, conv_ref, cot_ref, maskf, gain_ref, bias_ref, act_ref, dpre_ref, par_ref, sum_ref, tmp
):
    batch, chans, _ = conv_ref.shape
    high, width = maskf.shape
    stat = stat_ref[:, 0, :]
    n = stat_ref[:, 1, :]
    count = jnp.maximum(jnp.sum(n, axis=0, keepdims=True), 1.0)
    both = jnp.sum(stat, axis=0, keepdims=True)
    mean = both / count
    off = stat / jnp.maximum(n, 1.0) - mean
    between = jnp.sum(n * off * off, axis=0, keepdims=True)
    var = (rolled(both, chans, width) + between) / count
    inv = lax.rsqrt(var + EPS)
    gain = widened(gain_ref[...], width)
    bias = widened(bias_ref[...], width)
    cols = columns([mean, inv, gain, 0.5 * gain * inv, 0.5 * bias, count], chans)
    par_ref[...] = cols
    mean, slope, shift = (column(cols, k, width) for k in (0, 3, 4))
    sums = (jnp.zeros((chans, width), F32), jnp.zeros((chans, width), F32))
    for b in range(batch):

        def row(h, sums, b=b):
            at = row_lanes(h, width)
            dev = conv_ref[b, :, at] - mean
            half = slope * dev + shift
            t = jnp.tanh(half)
            s = 0.5 + 0.5 * t
            act = half + half * t
            tmp[channel_rows(b, h, chans, high), :] = act * maskf[pl.ds(h, 1), :]
            dpre = cot_ref[b, :, at].astype(F32) * (s + act * (0.5 - 0.5 * t))
            dpre_ref[b, :, at] = dpre
            return sums[0] + dpre, sums[1] + dpre * dev

        sums = lax.fori_loop(0, high, row, sums, unroll=4)
    total = lanes_sum(sums[0], sums[1] * column(cols, 1, width))
    sum_ref[...] = jnp.broadcast_to(total[None], sum_ref.shape)
    for b in range(batch):
        pack_rows(tmp.at[b * chans * (high + 1) : (b + 1) * chans * (high + 1)], act_ref.at[b], chans, high)


def grad_kernel(
    sum_ref, conv_ref, dpre_ref, par_ref, pad_ref, stack_ref, maskf,
    d_ref, top_ref, bot_ref, side_ref, out_ref, bg_ref, gg_ref, acc, wg_ref, *bufs,
):
    batch, chans, _ = conv_ref.shape
    high, width = maskf.shape
    lane = lane_of(chans, width)
    both = jnp.sum(sum_ref[:, 0, :], axis=0, keepdims=True)
    bg_ref[...] = both[:, 0:chans]
    gg_ref[...] = both[:, chans : 2 * chans]
    cols = par_ref[...]
    mean, inv, gain, count = (column(cols, k, width) for k in (0, 1, 2, 5))
    sums = columns([both], 2 * chans)
    scale = gain * inv
    first = scale * column(sums[0:chans], 0, width) / count
    second = scale * inv * column(sums[chans:], 0, width) / count
    acc[...] = jnp.zeros_like(acc)
    contract = (((1,), (1,)), ((), ()))
    per = high // GROUP
    steps = batch * per

    def place(k):
        return lax.div(k, per), lax.rem(k, per) * GROUP

    def build(k, buf, side):
        b, j = place(k)
        for r in range(GROUP):
            h = j + r
            at = row_lanes(h, width)
            dev = conv_ref[b, :, at] - mean
            d = (maskf[pl.ds(h, 1), :] * (scale * dpre_ref[b, :, at] - first - dev * second)).astype(BF16)
            d_ref[b, :, at] = d
            v = d.astype(F32)
            side = packed(side, v, b * high + h, lane)
            cut = slice(r * width, (r + 1) * width)
            buf[0:chans, cut] = jnp.where(lane == width - 1, 0.0, rolled(v, -1, width)).astype(BF16)
            buf[chans : 2 * chans, cut] = d
            buf[2 * chans :, cut] = jnp.where(lane == 0, 0.0, rolled(v, 1, width)).astype(BF16)
        return side

    def product(k, buf):
        b, j = place(k)
        return lax.dot_general(
            taps(pad_ref, b, j, width, GROUP), buf[...], contract, preferred_element_type=F32
        )

    def four(p, side):
        k = 4 * p
        gain = product(k, bufs[0]) + product(k + 1, bufs[1])
        side = build(k + 2, bufs[2], side)
        side = build(k + 3, bufs[3], side)
        acc[...] += gain
        gain = product(k + 2, bufs[2]) + product(k + 3, bufs[3])
        side = build(jnp.minimum(k + 4, steps - 1), bufs[0], side)
        side = build(jnp.minimum(k + 5, steps - 1), bufs[1], side)
        acc[...] += gain
        return side

    side = build(0, bufs[0], jnp.zeros((chans, width), F32))
    side = build(1, bufs[1], side)
    side = lax.fori_loop(0, steps // 4, four, side)
    for b in range(batch):
        top_ref[b] = d_ref[b, :, 0:width]
        bot_ref[b] = d_ref[b, :, (high - 1) * width : high * width]
    side_ref[...] = side.astype(BF16)
    even = lax.rem(lane, 2) == 0
    zero = jnp.zeros((chans, width), F32)
    rim = jnp.concatenate([jnp.where(even, side, 0.0), zero, jnp.where(even, 0.0, side)], axis=0)
    full = acc[...] + lax.dot_general(
        stack_ref[...], rim.astype(BF16), contract, preferred_element_type=F32
    )
    half = 3 * chans // 2
    wg_ref[0 : 3 * chans, :] = full[:, 0 : 2 * chans]
    wg_ref[3 * chans : 3 * chans + half, :] = jnp.concatenate(
        [full[0:half, 2 * chans :], full[half:, 2 * chans :]], axis=1
    )
    if wg_ref.shape[0] > 3 * chans + half:
        wg_ref[3 * chans + half :, :] = jnp.zeros((wg_ref.shape[0] - 3 * chans - half, width), F32)
    share = out_ref.shape[2] // width
    for p in range(out_ref.shape[0]):
        for r in range(share):
            out_ref[p, :, r * width : (r + 1) * width] = wg_ref[p * share + r : p * share + r + 1, :]


def unpack_kernel(chans, x_ref, out_ref, wg_ref):
    half = 3 * chans // 2
    width = wg_ref.shape[1]
    share = x_ref.shape[2] // width
    for p in range(x_ref.shape[0]):
        for r in range(share):
            wg_ref[p * share + r : p * share + r + 1, :] = x_ref[p, :, r * width : (r + 1) * width]
    for ky in range(3):
        for kx in range(2):
            out_ref[ky, kx] = wg_ref[ky * chans : (ky + 1) * chans, kx * chans : (kx + 1) * chans]
    tail = jnp.concatenate(
        [
            wg_ref[3 * chans : 3 * chans + half, 0:chans],
            wg_ref[3 * chans : 3 * chans + half, chans : 2 * chans],
        ],
        axis=0,
    )
    for ky in range(3):
        out_ref[ky, 2] = tail[ky * chans : (ky + 1) * chans]


def back_kernel(plane, d_ref, above_ref, below_ref, edge_ref, w_ref, maskf, *rest):
    out_ref, pad_ref, tmp, *bufs, tile, sem = rest[-9:]
    batch, chans, _ = d_ref.shape
    high, width = maskf.shape
    lane = lane_of(chans, width)
    fill_padded(pad_ref, d_ref, above_ref, below_ref, width, [plane])
    stack = edge_stack(edge_ref[...].astype(F32), above_ref[batch], below_ref[batch], high, batch)
    fix = edge_fix(w_ref, stack, lane)

    def post(b, h, value, carry):
        tmp[channel_rows(0, h, chans, high), :] = value * maskf[pl.ds(h, 1), :]
        return carry

    conv_loop(pad_ref, w_ref, bufs, fix, plane, high, lane, post, 0)
    pack_rows(tmp, tile, chans, high)
    copy = pltpu.make_async_copy(tile, out_ref.at[plane], sem)
    copy.start()
    copy.wait()


def neighbours(axis, ring):
    n = lax.axis_size(axis)
    even = [(i, i ^ 1) for i in range(n)]
    odd = [(i, (i + 1) % n if i % 2 else (i - 1) % n) for i in range(n)]
    if not ring:
        odd = [pair for pair in odd if pair not in ((0, n - 1), (n - 1, 0))]
    return even, odd


def lon_swap(side):
    n = lax.axis_size("lon")
    if n % 2:
        from_left = lax.ppermute(side, "lon", [(i, (i + 1) % n) for i in range(n)])
        from_right = lax.ppermute(side, "lon", [((i + 1) % n, i) for i in range(n)])
        return from_left, from_right
    even, odd = neighbours("lon", True)
    first = lax.ppermute(side, "lon", even)
    second = lax.ppermute(side, "lon", odd)
    flag = lax.axis_index("lon") % 2 == 1
    return jnp.where(flag, first, second), jnp.where(flag, second, first)


def lat_swap(up, dn):
    n = lax.axis_size("lat")
    if n % 2:
        above = lax.ppermute(dn, "lat", [(i, i + 1) for i in range(n - 1)])
        below = lax.ppermute(up, "lat", [(i + 1, i) for i in range(n - 1)])
        return above, below
    even, odd = neighbours("lat", False)
    flag = lax.axis_index("lat") % 2 == 1
    second = lax.ppermute(jnp.where(flag, dn, up), "lat", odd)
    first = lax.ppermute(jnp.where(flag, up, dn), "lat", even)
    return jnp.where(flag, first, second), jnp.where(flag, second, first)


def with_corners(side, above, below, high):
    shape = jax.ShapeDtypeStruct((2,) + side.shape, BF16)
    return call(functools.partial(corner_kernel, high), shape, [], 0, 200_000, side, above, below)


def with_poles(top, bot, sides, high):
    batch, chans, width = top.shape
    shapes = (
        jax.ShapeDtypeStruct((chans, width), BF16),
        jax.ShapeDtypeStruct((batch + 1, chans, width), BF16),
        jax.ShapeDtypeStruct((batch + 1, chans, width), BF16),
    )
    return call(functools.partial(pole_kernel, high, batch), shapes, [], 0, 200_000, top, bot, *sides)


def on_device(state, land_mask, conv_weight, norm_gain, batchnorm_bias, cotangent):
    batch, chans, high, width = state.shape
    flat = high * width
    axes = ("lat", "lon")
    devices = lax.axis_size(axes)
    S = jax.ShapeDtypeStruct
    mat = 2 * batch * flat * 9 * chans * chans
    size = batch * chans * flat * 2
    tmp = pltpu.VMEM((batch * chans * (high + 1), width), F32)
    products = [pltpu.VMEM((3 * chans, STEP * width), F32)] * 4
    plane = S((batch, chans, flat), BF16)
    wide = S((batch, chans, flat), F32)
    rows = S((batch, chans, width), BF16)
    cols = S((chans, width), BF16)
    square = S((3 * chans, 3 * chans), BF16)
    top, bot, flag = call(
        ends_kernel, (rows, rows, S((high, width), F32)), [pltpu.VMEM((chans, width), F32)], 0, size // 8,
        state, land_mask,
    )
    above, below = lat_swap(top, bot)
    xm, side = call(gather_kernel, (plane, cols), [tmp], 0, 2 * size, state, flag)
    cot, w_fwd, w_back = call(
        relay_kernel, (plane, square, square), [tmp], 0, 2 * size, cotangent, flag, conv_weight
    )
    left, right = lon_swap(with_corners(side, above, below, high))
    conv, padded, stack, stat = call(
        conv_kernel,
        (
            wide,
            S((batch, chans, flat + 2 * width), BF16),
            S((3 * chans, width), BF16),
            S((devices, 2, 2 * chans), F32),
        ),
        products,
        4 * mat,
        4 * size,
        xm, above, below, left, right, w_fwd, flag,
    )
    stats = lax.all_to_all(stat, axes, 0, 0)
    activated, dpre, par, sums = call(
        silu_kernel,
        (S(state.shape, BF16), wide, S((chans, width), F32), S((devices, 1, 2 * chans), F32)),
        [tmp],
        20 * size,
        6 * size,
        stats, conv, cot, flag, norm_gain[None], batchnorm_bias[None],
    )
    sums = lax.all_to_all(sums, axes, 0, 0)
    stacked = pltpu.VMEM((3 * chans, GROUP * width), BF16)
    share = -(-9 * chans * chans // (width * devices))
    flatg = pltpu.VMEM((share * devices, width), F32)
    dmap, top, bot, side, wg, bg, gg = call(
        grad_kernel,
        (
            plane, rows, rows, cols,
            S((devices, 1, share * width), F32), S((1, chans), F32), S((1, chans), F32),
        ),
        [pltpu.VMEM((3 * chans, 3 * chans), F32), flatg, stacked, stacked, stacked, stacked],
        4 * mat,
        6 * size,
        sums, conv, dpre, par, padded, stack, flag,
    )

    parts = lax.all_to_all(wg, axes, 0, 0)
    edge, up, dn = with_poles(top, bot, lon_swap(side), high)
    above, below = lat_swap(up, dn)
    parts, above, below, edge = lax.optimization_barrier((parts, above, below, edge))
    shares = jnp.broadcast_to(jnp.sum(parts, axis=0, keepdims=True), parts.shape)
    wg = lax.all_to_all(shares, axes, 0, 0)

    def backward(b, earlier):
        kept = {} if earlier is None else {"input_output_aliases": {6: 0}}
        whole = pl.BlockSpec(memory_space=pltpu.VMEM)
        far = pl.BlockSpec(memory_space=pl.ANY)
        extra = [] if earlier is None else [earlier]
        return pl.pallas_call(
            functools.partial(back_kernel, b),
            out_shape=S(state.shape, BF16),
            in_specs=[whole] * 6 + [far] * len(extra),
            out_specs=far,
            scratch_shapes=[
                pltpu.VMEM((1, chans, flat + 2 * width), BF16),
                pltpu.VMEM((chans * (high + 1), width), F32),
            ]
            + products
            + [pltpu.VMEM((chans, high, width), BF16), pltpu.SemaphoreType.DMA],
            compiler_params=pltpu.CompilerParams(vmem_limit_bytes=24 << 20),
            cost_estimate=pl.CostEstimate(flops=2 * mat, bytes_accessed=2 * size, transcendentals=0),
            **kept,
        )(dmap, above, below, edge, w_back, flag, *extra)

    state_grad = None
    for b in range(batch):
        state_grad = backward(b, state_grad)
    weight_grad = call(
        functools.partial(unpack_kernel, chans), S((3, 3, chans, chans), F32), [flatg], 0, 500_000, wg
    )
    return (activated, state_grad, weight_grad, gg[0], bg[0])


def solution(mesh):
    return jax.shard_map(
        on_device,
        mesh=mesh,
        in_specs=(
            P(None, None, "lat", "lon"),
            P("lat", "lon"),
            P(),
            P(),
            P(),
            P(None, None, "lat", "lon"),
        ),
        out_specs=(P(None, None, "lat", "lon"), P(None, None, "lat", "lon"), P(), P(), P()),
        check_vma=False,
    )
```

```python
import functools

import jax
import jax.numpy as jnp
from jax import lax
from jax.experimental import pallas as pl
from jax.experimental.pallas import tpu as pltpu
from jax.sharding import PartitionSpec as P


F32 = jnp.float32
BF16 = jnp.bfloat16
STEP = 2
GROUP = 4
EPS = 1e-05


def lane_of(rows, width):
    return lax.broadcasted_iota(jnp.int32, (rows, width), 1)


def rolled(value, shift, width):
    return pltpu.roll(value, lax.rem(shift + 4 * width, width), 1)


def any_lane(lane, picks):
    hit = lane == picks[0]
    for p in picks[1:]:
        hit = jnp.logical_or(hit, lane == p)
    return hit


def call(kernel, out_shape, scratch, flops, nbytes, *args):
    return pl.pallas_call(
        kernel,
        out_shape=out_shape,
        in_specs=[pl.BlockSpec(memory_space=pltpu.VMEM)] * len(args),
        scratch_shapes=scratch,
        compiler_params=pltpu.CompilerParams(vmem_limit_bytes=24 << 20),
        cost_estimate=pl.CostEstimate(flops=flops, bytes_accessed=nbytes, transcendentals=0),
    )(*args)


def row_lanes(h, width, count=1):
    return pl.ds(pl.multiple_of(h * width, width), count * width)


def spread_rows(src_ref, tmp, mask):
    batch, chans, high, _ = src_ref.shape
    for b in range(batch):
        for c in range(chans):
            at = (b * chans + c) * (high + 1)
            tmp[at : at + high, :] = src_ref[b, c].astype(F32) * mask


def channel_rows(b, h, chans, high):
    return pl.ds(b * chans * (high + 1) + h, chans, stride=high + 1)


def pack_rows(tmp, out, chans, high):
    for c in range(chans):
        at = c * (high + 1)
        out[c] = tmp[at : at + high, :].astype(BF16)


def packed(old, v, i, lane):
    width = lane.shape[1]
    here = jnp.logical_or(lane == 2 * i, lane == lax.rem(2 * i - 1 + width, width))
    return jnp.where(here, rolled(v, 2 * i, width), old)


def ends_kernel(x_ref, mask_ref, top_ref, bot_ref, maskf, tmp):
    batch, chans, high, _ = x_ref.shape
    maskf[...] = mask_ref[...].astype(F32)
    for h, out_ref in ((0, top_ref), (high - 1, bot_ref)):
        base = h - h % 16
        for b in range(batch):
            for c in range(chans):
                tile = x_ref[b, c, base : base + 16].astype(F32)
                tmp[c : c + 1, :] = tile[h - base : h - base + 1]
            out_ref[b] = (tmp[...] * maskf[h : h + 1, :]).astype(BF16)


def gather_kernel(x_ref, maskf, xm_ref, side_ref, tmp):
    batch, chans, high, width = x_ref.shape
    spread_rows(x_ref, tmp, maskf[...])
    lane = lane_of(chans, width)
    side = jnp.zeros((chans, width), F32)
    for b in range(batch):

        def row(h, side, b=b):
            v = tmp[channel_rows(b, h, chans, high), :]
            xm_ref[b, :, row_lanes(h, width)] = v.astype(BF16)
            return packed(side, v, b * high + h, lane)

        side = lax.fori_loop(0, high, row, side, unroll=8)
    side_ref[...] = side.astype(BF16)


def relay_kernel(x_ref, maskf, w_ref, out_ref, fwd_ref, back_ref, tmp):
    batch, chans, high, width = x_ref.shape
    spread_rows(x_ref, tmp, maskf[...])
    for kx in range(3):
        part = jnp.concatenate([w_ref[ky, kx].astype(F32) for ky in range(3)], axis=0)
        fwd_ref[kx * chans : (kx + 1) * chans, :] = jnp.transpose(part).astype(BF16)
        part = [w_ref[2 - ky, 2 - kx].astype(F32) for ky in range(3)]
        back_ref[kx * chans : (kx + 1) * chans, :] = jnp.concatenate(part, axis=1).astype(BF16)
    for b in range(batch):

        def row(h, carry, b=b):
            out_ref[b, :, row_lanes(h, width)] = tmp[channel_rows(b, h, chans, high), :].astype(BF16)
            return carry

        lax.fori_loop(0, high, row, 0, unroll=8)


def corners(high, batch, width):
    first = [(2 * b * high + d) % width for b in range(batch) for d in (0, -1)]
    return first, [(p + 2 * (high - 1)) % width for p in first]


def corner_kernel(high, side_ref, above_ref, below_ref, out_ref):
    chans, width = side_ref.shape
    lane = lane_of(chans, width)
    pack = jnp.zeros((chans, width), F32)
    for b in range(above_ref.shape[0]):
        pack = packed(pack, above_ref[b].astype(F32), b * high, lane)
        pack = packed(pack, below_ref[b].astype(F32), b * high + high - 1, lane)
    out_ref[0] = side_ref[...]
    out_ref[1] = pack.astype(BF16)


def pole_kernel(high, batch, top_ref, bot_ref, fl_ref, fr_ref, edge_ref, up_ref, dn_ref):
    chans, width = fl_ref.shape
    lane = lane_of(chans, width)
    even = lax.rem(lane, 2) == 0
    edge = jnp.where(
        even, rolled(fl_ref[...].astype(F32), 1, width), rolled(fr_ref[...].astype(F32), -1, width)
    )
    first, last = corners(high, batch, width)
    far = 2 * (high - 1)
    edge_ref[...] = edge.astype(BF16)
    up = jnp.where(any_lane(lane, last), rolled(edge, far, width), 0.0)
    dn = jnp.where(any_lane(lane, first), rolled(edge, -far, width), 0.0)
    for b in range(batch):
        up_ref[b] = top_ref[b]
        dn_ref[b] = bot_ref[b]
    up_ref[batch] = up.astype(BF16)
    dn_ref[batch] = dn.astype(BF16)


def facing(left, right):
    chans, width = left.shape
    even = lax.rem(lane_of(chans, width), 2) == 0
    return jnp.where(even, rolled(left.astype(F32), 1, width), rolled(right.astype(F32), -1, width))


def edge_stack(edge, above, below, high, batch):
    chans, width = edge.shape
    lane = lane_of(chans, width)
    first, last = corners(high, batch, width)
    top = jnp.where(any_lane(lane, first), above.astype(F32), rolled(edge, 2, width))
    bottom = jnp.where(any_lane(lane, last), below.astype(F32), rolled(edge, -2, width))
    return jnp.concatenate([top, edge, bottom], axis=0).astype(BF16)


def fill_padded(pad_ref, x_ref, above_ref, below_ref, width, planes):
    flat = x_ref.shape[2]
    for to, b in enumerate(planes):
        pad_ref[to, :, 0:width] = above_ref[b]
        pad_ref[to, :, width : width + flat] = x_ref[b]
        pad_ref[to, :, width + flat :] = below_ref[b]


def taps(pad_ref, b, j, width, count):
    return jnp.concatenate([pad_ref[b, :, row_lanes(j + ky, width, count)] for ky in range(3)], axis=0)


def edge_fix(w_ref, stack, lane):
    g = jnp.dot(w_ref[...], stack, preferred_element_type=F32)
    c = g.shape[0] // 3
    return jnp.where(lax.rem(lane, 2) == 0, g[0:c], g[2 * c :])


def conv_loop(pad_ref, w_ref, bufs, fix, first, high, lane, post, carry):
    planes = pad_ref.shape[0]
    chans, width = lane.shape
    per = high // STEP
    steps = planes * per

    def product(k, buf):
        k = jnp.minimum(k, steps - 1)
        b, j = lax.div(k, per), lax.rem(k, per) * STEP
        buf[...] = jnp.dot(w_ref[...], taps(pad_ref, b, j, width, STEP), preferred_element_type=F32)

    def finish(k, buf, carry):
        b, j = lax.div(k, per), lax.rem(k, per) * STEP
        for r in range(STEP):
            cut = slice(r * width, (r + 1) * width)
            g = rolled(fix, -2 * ((first + b) * high + j + r), width)
            left = jnp.where(lane == 0, g, rolled(buf[0:chans, cut], 1, width))
            right = jnp.where(lane == width - 1, g, rolled(buf[2 * chans :, cut], -1, width))
            carry = post(b, j + r, left + buf[chans : 2 * chans, cut] + right, carry)
        return carry

    def four(p, carry):
        k = 4 * p
        product(k + 2, bufs[2])
        product(k + 3, bufs[3])
        carry = finish(k, bufs[0], carry)
        carry = finish(k + 1, bufs[1], carry)
        product(k + 4, bufs[0])
        product(k + 5, bufs[1])
        carry = finish(k + 2, bufs[2], carry)
        return finish(k + 3, bufs[3], carry)

    product(0, bufs[0])
    product(1, bufs[1])
    return lax.fori_loop(0, steps // 4, four, carry)


def lanes_sum(first, second):
    both = jnp.concatenate([first, second], axis=0)
    return jnp.sum(jnp.transpose(both), axis=0, keepdims=True)


def conv_kernel(
    x_ref, above_ref, below_ref, left_ref, right_ref, w_ref, maskf,
    conv_ref, pad_ref, stack_ref, stat_ref, *bufs,
):
    batch, chans, _ = x_ref.shape
    high, width = maskf.shape
    lane = lane_of(chans, width)
    fill_padded(pad_ref, x_ref, above_ref, below_ref, width, range(batch))
    corner = facing(left_ref[1], right_ref[1])
    stack = edge_stack(facing(left_ref[0], right_ref[0]), corner, corner, high, batch)
    stack_ref[...] = stack
    fix = edge_fix(w_ref, stack, lane)

    def post(b, h, value, total):
        conv_ref[b, :, row_lanes(h, width)] = value
        return total + value * maskf[pl.ds(h, 1), :]

    zero = jnp.zeros((chans, width), F32)
    total = conv_loop(pad_ref, w_ref, bufs, fix, 0, high, lane, post, zero)
    n = batch * jnp.sum(maskf[...])
    mean = jnp.sum(total, axis=1, keepdims=True) / jnp.maximum(n, 1.0)
    mean = jnp.broadcast_to(mean, (chans, width))
    spread = zero
    for b in range(batch):

        def step(h, spread, b=b):
            dev = conv_ref[b, :, row_lanes(h, width)] - mean
            return spread + dev * dev * maskf[pl.ds(h, 1), :]

        spread = lax.fori_loop(0, high, step, spread, unroll=8)
    copies = stat_ref.shape[0]
    stat_ref[:, 0:1, :] = jnp.broadcast_to(lanes_sum(total, spread)[None], (copies, 1, 2 * chans))
    stat_ref[:, 1:2, :] = jnp.full((copies, 1, 2 * chans), n, F32)


def columns(rows, chans):
    width = rows[0].shape[1]
    pad = jnp.zeros((width - len(rows), width), F32)
    return jnp.transpose(jnp.concatenate(rows + [pad], axis=0))[0:chans]


def column(cols, k, width):
    return jnp.broadcast_to(cols[:, k : k + 1], (cols.shape[0], width))


def widened(row, width):
    return jnp.concatenate([row, jnp.zeros((1, width - row.shape[1]), F32)], axis=1)


def silu_kernel(
    stat_ref, conv_ref, cot_ref, maskf, gain_ref, bias_ref, act_ref, dpre_ref, par_ref, sum_ref
):
    batch, chans, _ = conv_ref.shape
    high, width = maskf.shape
    stat = stat_ref[:, 0, :]
    n = stat_ref[:, 1, :]
    count = jnp.maximum(jnp.sum(n, axis=0, keepdims=True), 1.0)
    both = jnp.sum(stat, axis=0, keepdims=True)
    mean = both / count
    off = stat / jnp.maximum(n, 1.0) - mean
    between = jnp.sum(n * off * off, axis=0, keepdims=True)
    var = (rolled(both, chans, width) + between) / count
    inv = lax.rsqrt(var + EPS)
    gain = widened(gain_ref[...], width)
    bias = widened(bias_ref[...], width)
    cols = columns([mean, inv, gain, 0.5 * gain * inv, 0.5 * bias, count], chans)
    par_ref[...] = cols
    mean, slope, shift = (column(cols, k, width) for k in (0, 3, 4))
    sums = (jnp.zeros((chans, width), F32), jnp.zeros((chans, width), F32))
    for b in range(batch):

        def row(h, sums, b=b):
            at = row_lanes(h, width)
            dev = conv_ref[b, :, at] - mean
            half = slope * dev + shift
            t = jnp.tanh(half)
            s = 0.5 + 0.5 * t
            act = half + half * t
            act_ref[b, :, at] = (act * maskf[pl.ds(h, 1), :]).astype(BF16)
            dpre = cot_ref[b, :, at].astype(F32) * (s + act * (0.5 - 0.5 * t))
            dpre_ref[b, :, at] = dpre
            return sums[0] + dpre, sums[1] + dpre * dev

        sums = lax.fori_loop(0, high, row, sums, unroll=4)
    total = lanes_sum(sums[0], sums[1] * column(cols, 1, width))
    sum_ref[...] = jnp.broadcast_to(total[None], sum_ref.shape)


def pack_kernel(act_ref, out_ref, tmp):
    batch, chans, high, width = out_ref.shape
    for b in range(batch):

        def row(h, carry, b=b):
            tmp[channel_rows(b, h, chans, high), :] = act_ref[b, :, row_lanes(h, width)].astype(F32)
            return carry

        lax.fori_loop(0, high, row, 0, unroll=8)
        pack_rows(tmp.at[b * chans * (high + 1) : (b + 1) * chans * (high + 1)], out_ref.at[b], chans, high)


def grad_kernel(
    sum_ref, conv_ref, dpre_ref, par_ref, pad_ref, stack_ref, maskf,
    d_ref, top_ref, bot_ref, side_ref, out_ref, bg_ref, gg_ref, acc, wg_ref, *bufs,
):
    batch, chans, _ = conv_ref.shape
    high, width = maskf.shape
    lane = lane_of(chans, width)
    both = jnp.sum(sum_ref[:, 0, :], axis=0, keepdims=True)
    bg_ref[...] = both[:, 0:chans]
    gg_ref[...] = both[:, chans : 2 * chans]
    cols = par_ref[...]
    mean, inv, gain, count = (column(cols, k, width) for k in (0, 1, 2, 5))
    sums = columns([both], 2 * chans)
    scale = gain * inv
    first = scale * column(sums[0:chans], 0, width) / count
    second = scale * inv * column(sums[chans:], 0, width) / count
    acc[...] = jnp.zeros_like(acc)
    contract = (((1,), (1,)), ((), ()))
    per = high // GROUP
    steps = batch * per

    def place(k):
        return lax.div(k, per), lax.rem(k, per) * GROUP

    def build(k, buf, side):
        b, j = place(k)
        for r in range(GROUP):
            h = j + r
            at = row_lanes(h, width)
            dev = conv_ref[b, :, at] - mean
            d = (maskf[pl.ds(h, 1), :] * (scale * dpre_ref[b, :, at] - first - dev * second)).astype(BF16)
            d_ref[b, :, at] = d
            v = d.astype(F32)
            side = packed(side, v, b * high + h, lane)
            cut = slice(r * width, (r + 1) * width)
            buf[0:chans, cut] = jnp.where(lane == width - 1, 0.0, rolled(v, -1, width)).astype(BF16)
            buf[chans : 2 * chans, cut] = d
            buf[2 * chans :, cut] = jnp.where(lane == 0, 0.0, rolled(v, 1, width)).astype(BF16)
        return side

    def product(k, buf):
        b, j = place(k)
        return lax.dot_general(
            taps(pad_ref, b, j, width, GROUP), buf[...], contract, preferred_element_type=F32
        )

    def four(p, side):
        k = 4 * p
        gain = product(k, bufs[0]) + product(k + 1, bufs[1])
        side = build(k + 2, bufs[2], side)
        side = build(k + 3, bufs[3], side)
        acc[...] += gain
        gain = product(k + 2, bufs[2]) + product(k + 3, bufs[3])
        side = build(jnp.minimum(k + 4, steps - 1), bufs[0], side)
        side = build(jnp.minimum(k + 5, steps - 1), bufs[1], side)
        acc[...] += gain
        return side

    side = build(0, bufs[0], jnp.zeros((chans, width), F32))
    side = build(1, bufs[1], side)
    side = lax.fori_loop(0, steps // 4, four, side)
    for b in range(batch):
        top_ref[b] = d_ref[b, :, 0:width]
        bot_ref[b] = d_ref[b, :, (high - 1) * width : high * width]
    side_ref[...] = side.astype(BF16)
    even = lax.rem(lane, 2) == 0
    zero = jnp.zeros((chans, width), F32)
    rim = jnp.concatenate([jnp.where(even, side, 0.0), zero, jnp.where(even, 0.0, side)], axis=0)
    full = acc[...] + lax.dot_general(
        stack_ref[...], rim.astype(BF16), contract, preferred_element_type=F32
    )
    half = 3 * chans // 2
    wg_ref[0 : 3 * chans, :] = full[:, 0 : 2 * chans]
    wg_ref[3 * chans : 3 * chans + half, :] = jnp.concatenate(
        [full[0:half, 2 * chans :], full[half:, 2 * chans :]], axis=1
    )
    if wg_ref.shape[0] > 3 * chans + half:
        wg_ref[3 * chans + half :, :] = jnp.zeros((wg_ref.shape[0] - 3 * chans - half, width), F32)
    share = out_ref.shape[2] // width
    for p in range(out_ref.shape[0]):
        for r in range(share):
            out_ref[p, :, r * width : (r + 1) * width] = wg_ref[p * share + r : p * share + r + 1, :]


def unpack_kernel(chans, x_ref, out_ref, wg_ref):
    half = 3 * chans // 2
    width = wg_ref.shape[1]
    share = x_ref.shape[2] // width
    for p in range(x_ref.shape[0]):
        for r in range(share):
            wg_ref[p * share + r : p * share + r + 1, :] = x_ref[p, :, r * width : (r + 1) * width]
    for ky in range(3):
        for kx in range(2):
            out_ref[ky, kx] = wg_ref[ky * chans : (ky + 1) * chans, kx * chans : (kx + 1) * chans]
    tail = jnp.concatenate(
        [
            wg_ref[3 * chans : 3 * chans + half, 0:chans],
            wg_ref[3 * chans : 3 * chans + half, chans : 2 * chans],
        ],
        axis=0,
    )
    for ky in range(3):
        out_ref[ky, 2] = tail[ky * chans : (ky + 1) * chans]


def back_kernel(plane, d_ref, above_ref, below_ref, edge_ref, w_ref, maskf, *rest):
    out_ref, pad_ref, tmp, *bufs, tile, sem = rest[-9:]
    batch, chans, _ = d_ref.shape
    high, width = maskf.shape
    lane = lane_of(chans, width)
    fill_padded(pad_ref, d_ref, above_ref, below_ref, width, [plane])
    stack = edge_stack(edge_ref[...].astype(F32), above_ref[batch], below_ref[batch], high, batch)
    fix = edge_fix(w_ref, stack, lane)

    def post(b, h, value, carry):
        tmp[channel_rows(0, h, chans, high), :] = value * maskf[pl.ds(h, 1), :]
        return carry

    conv_loop(pad_ref, w_ref, bufs, fix, plane, high, lane, post, 0)
    pack_rows(tmp, tile, chans, high)
    copy = pltpu.make_async_copy(tile, out_ref.at[plane], sem)
    copy.start()
    copy.wait()


def neighbours(axis, ring):
    n = lax.axis_size(axis)
    even = [(i, i ^ 1) for i in range(n)]
    odd = [(i, (i + 1) % n if i % 2 else (i - 1) % n) for i in range(n)]
    if not ring:
        odd = [pair for pair in odd if pair not in ((0, n - 1), (n - 1, 0))]
    return even, odd


def lon_swap(side):
    n = lax.axis_size("lon")
    if n % 2:
        from_left = lax.ppermute(side, "lon", [(i, (i + 1) % n) for i in range(n)])
        from_right = lax.ppermute(side, "lon", [((i + 1) % n, i) for i in range(n)])
        return from_left, from_right
    even, odd = neighbours("lon", True)
    first = lax.ppermute(side, "lon", even)
    second = lax.ppermute(side, "lon", odd)
    flag = lax.axis_index("lon") % 2 == 1
    return jnp.where(flag, first, second), jnp.where(flag, second, first)


def lat_swap(up, dn):
    n = lax.axis_size("lat")
    if n % 2:
        above = lax.ppermute(dn, "lat", [(i, i + 1) for i in range(n - 1)])
        below = lax.ppermute(up, "lat", [(i + 1, i) for i in range(n - 1)])
        return above, below
    even, odd = neighbours("lat", False)
    flag = lax.axis_index("lat") % 2 == 1
    second = lax.ppermute(jnp.where(flag, dn, up), "lat", odd)
    first = lax.ppermute(jnp.where(flag, up, dn), "lat", even)
    return jnp.where(flag, first, second), jnp.where(flag, second, first)


def with_corners(side, above, below, high):
    shape = jax.ShapeDtypeStruct((2,) + side.shape, BF16)
    return call(functools.partial(corner_kernel, high), shape, [], 0, 200_000, side, above, below)


def with_poles(top, bot, sides, high):
    batch, chans, width = top.shape
    shapes = (
        jax.ShapeDtypeStruct((chans, width), BF16),
        jax.ShapeDtypeStruct((batch + 1, chans, width), BF16),
        jax.ShapeDtypeStruct((batch + 1, chans, width), BF16),
    )
    return call(functools.partial(pole_kernel, high, batch), shapes, [], 0, 200_000, top, bot, *sides)


def on_device(state, land_mask, conv_weight, norm_gain, batchnorm_bias, cotangent):
    batch, chans, high, width = state.shape
    flat = high * width
    axes = ("lat", "lon")
    devices = lax.axis_size(axes)
    S = jax.ShapeDtypeStruct
    mat = 2 * batch * flat * 9 * chans * chans
    size = batch * chans * flat * 2
    tmp = pltpu.VMEM((batch * chans * (high + 1), width), F32)
    products = [pltpu.VMEM((3 * chans, STEP * width), F32)] * 4
    plane = S((batch, chans, flat), BF16)
    wide = S((batch, chans, flat), F32)
    rows = S((batch, chans, width), BF16)
    cols = S((chans, width), BF16)
    square = S((3 * chans, 3 * chans), BF16)
    top, bot, flag = call(
        ends_kernel, (rows, rows, S((high, width), F32)), [pltpu.VMEM((chans, width), F32)], 0, size // 8,
        state, land_mask,
    )
    above, below = lat_swap(top, bot)
    xm, side = call(gather_kernel, (plane, cols), [tmp], 0, 2 * size, state, flag)
    cot, w_fwd, w_back = call(
        relay_kernel, (plane, square, square), [tmp], 0, 2 * size, cotangent, flag, conv_weight
    )
    left, right = lon_swap(with_corners(side, above, below, high))
    conv, padded, stack, stat = call(
        conv_kernel,
        (
            wide,
            S((batch, chans, flat + 2 * width), BF16),
            S((3 * chans, width), BF16),
            S((devices, 2, 2 * chans), F32),
        ),
        products,
        4 * mat,
        4 * size,
        xm, above, below, left, right, w_fwd, flag,
    )
    stats = lax.all_to_all(stat, axes, 0, 0)
    active, dpre, par, sums = call(
        silu_kernel,
        (plane, wide, S((chans, width), F32), S((devices, 1, 2 * chans), F32)),
        [],
        20 * size,
        6 * size,
        stats, conv, cot, flag, norm_gain[None], batchnorm_bias[None],
    )
    sums = lax.all_to_all(sums, axes, 0, 0)
    activated = call(pack_kernel, S(state.shape, BF16), [tmp], 0, 3 * size, active)
    stacked = pltpu.VMEM((3 * chans, GROUP * width), BF16)
    share = -(-9 * chans * chans // (width * devices))
    flatg = pltpu.VMEM((share * devices, width), F32)
    dmap, top, bot, side, wg, bg, gg = call(
        grad_kernel,
        (
            plane, rows, rows, cols,
            S((devices, 1, share * width), F32), S((1, chans), F32), S((1, chans), F32),
        ),
        [pltpu.VMEM((3 * chans, 3 * chans), F32), flatg, stacked, stacked, stacked, stacked],
        4 * mat,
        6 * size,
        sums, conv, dpre, par, padded, stack, flag,
    )

    parts = lax.all_to_all(wg, axes, 0, 0)
    edge, up, dn = with_poles(top, bot, lon_swap(side), high)
    above, below = lat_swap(up, dn)
    parts, above, below, edge = lax.optimization_barrier((parts, above, below, edge))
    shares = jnp.broadcast_to(jnp.sum(parts, axis=0, keepdims=True), parts.shape)
    wg = lax.all_to_all(shares, axes, 0, 0)

    def backward(b, earlier):
        kept = {} if earlier is None else {"input_output_aliases": {6: 0}}
        whole = pl.BlockSpec(memory_space=pltpu.VMEM)
        far = pl.BlockSpec(memory_space=pl.ANY)
        extra = [] if earlier is None else [earlier]
        return pl.pallas_call(
            functools.partial(back_kernel, b),
            out_shape=S(state.shape, BF16),
            in_specs=[whole] * 6 + [far] * len(extra),
            out_specs=far,
            scratch_shapes=[
                pltpu.VMEM((1, chans, flat + 2 * width), BF16),
                pltpu.VMEM((chans * (high + 1), width), F32),
            ]
            + products
            + [pltpu.VMEM((chans, high, width), BF16), pltpu.SemaphoreType.DMA],
            compiler_params=pltpu.CompilerParams(vmem_limit_bytes=24 << 20),
            cost_estimate=pl.CostEstimate(flops=2 * mat, bytes_accessed=2 * size, transcendentals=0),
            **kept,
        )(dmap, above, below, edge, w_back, flag, *extra)

    state_grad = None
    for b in range(batch):
        state_grad = backward(b, state_grad)
    weight_grad = call(
        functools.partial(unpack_kernel, chans), S((3, 3, chans, chans), F32), [flatg], 0, 500_000, wg
    )
    return (activated, state_grad, weight_grad, gg[0], bg[0])


def solution(mesh):
    return jax.shard_map(
        on_device,
        mesh=mesh,
        in_specs=(
            P(None, None, "lat", "lon"),
            P("lat", "lon"),
            P(),
            P(),
            P(),
            P(None, None, "lat", "lon"),
        ),
        out_specs=(P(None, None, "lat", "lon"), P(None, None, "lat", "lon"), P(), P(), P()),
        check_vma=False,
    )
```
